32 devices in a mesh: dp: 1, expert: 16 (over z, x, core), tensor: 2 (over y).
Axes of the slice: x: 2, y: 2, z: 4, core: 2. Of those that a mesh axis runs over, the one named last changes fastest.
Arguments:
- quant_tokens: bfloat16 [512, 5120], P(('dp', 'expert', 'tensor')), may hold values from -6 to 6
- token_scales: float32 [512, 40], P(('dp', 'expert', 'tensor')), may hold values from 0.2 to 2.5
- expert_ids: int32 [512, 6], P(('dp', 'expert', 'tensor')), may hold values from 0 to 15, all different within a row; in each aligned block of 32 rows (0 to 31, 32 to 63, ...) at most 13 rows name the same one
- gate_weights: bfloat16 [512, 6], P(('dp', 'expert', 'tensor')), may hold values from 0.049804688 to 1
- grad_out: bfloat16 [512, 5120], P(('dp', 'expert', 'tensor')), may hold values from -4 to 4
- w_in: bfloat16 [5120, 16, 2, 1536], P('dp', 'expert', None, 'tensor'), may hold values from -0.078125 to 0.078125
- w_out: bfloat16 [5120, 16, 1536], P('dp', 'expert', 'tensor'), may hold values from -0.15625 to 0.15625
Outputs:
- grad_tokens: bfloat16 [512, 5120], P(('dp', 'expert', 'tensor'))
- grad_gates: float32 [512, 6], P(('dp', 'expert', 'tensor'))
- grad_w_in: bfloat16 [5120, 16, 2, 1536], P('dp', 'expert', None, 'tensor')
- grad_w_out: bfloat16 [5120, 16, 1536], P('dp', 'expert', 'tensor')
The draws below stay inside these ranges and needn't reach their ends.
Inputs may be any that keep to these rules, and one draw needn't show every extreme that they name: `expert_ids`: each row names 6 different experts; in each aligned block of 32 rows (the tokens of one index pair of dp and expert) no expert is named by more than 13 rows, a bound that some block reaches.
All inputs are finite; a program needn't handle non-finite values.
Results may differ from the reference program's by a relative error of at most 0.012.
Values may be sent and summed in bfloat16 or wider, within the bound.
No kernel may reach another device: no remote copies, remote signals or barrier semaphores. Data moves between devices by JAX's collectives and lax.ppermute only.
A program may use at most 128 MiB of HBM per device.

```python
import math
import jax
import jax.numpy as jnp
import numpy as np
from jax import lax

D = 5120
HID = 1536
TOP = 6
NBLK = 40
EXPERTS = 16
BLK = 32
CAP = 13
TOKENS = 512
N_DP = 1
N_TENSOR = 2


def block_levels(rng, extent, cuts, low, top_value):
    def one(dim, parts):
        steps = jax.random.uniform(jax.random.fold_in(jax.random.fold_in(rng, 6), dim), (parts,), jnp.float32, low / len(cuts), top_value / len(cuts))
        return jnp.repeat(jnp.exp(steps), extent[dim] // parts).reshape((-1,) + (1,) * (len(extent) - dim - 1))

    factor_of = one(*cuts[0])
    for cut in cuts[1:]:
        factor_of = factor_of * one(*cut)
    return factor_of


def routed_block(own_key, own, number, rows, amount, top, most, skew):
    sequence = jax.random.permutation(own_key, amount)
    crowded, usual = load_shares(amount, rows * top, most, skew, True), load_shares(amount, rows * top, most, skew, False)
    places = jnp.arange(amount)

    def named(sizes, rotation):
        used = int((sizes > 0).sum())
        fixed = max(1, used // 4)
        passed = fixed + (places - fixed + rotation * (used - fixed)) % max(1, amount - fixed)
        return jnp.zeros((amount,), jnp.int32).at[sequence[jnp.where(places < fixed, places, passed)]].set(jnp.asarray(sizes, jnp.int32))

    sizes = jnp.where(number % 4 == 0, named(crowded, number // 4), named(usual, number - number // 4 - 1))
    mixed = jax.random.permutation(jax.random.fold_in(own, 3), amount)
    giver, taker = mixed[0:amount // 2 * 2:2], mixed[1:amount // 2 * 2:2]
    margin = jnp.minimum(sizes[giver] - 1, most - sizes[taker]) // 2
    margin = jnp.where((giver == sequence[0]) | (taker == sequence[0]) | (sizes[taker] == 0), 0, jnp.maximum(margin, 0))
    passed = jax.random.randint(jax.random.fold_in(own, 4), (amount // 2,), 0, 1 << 20) % (margin + 1)
    sizes = sizes.at[giver].add(-passed).at[taker].add(passed)
    labels = jnp.searchsorted(jnp.cumsum(sizes), jnp.arange(rows * top), side="right").astype(jnp.int32)
    table = labels.reshape(top, rows).T
    table = table[jax.random.permutation(jax.random.fold_in(own, 1), rows)]
    rotation = jax.random.randint(jax.random.fold_in(own, 2), (rows, 1), 0, top)
    return jnp.take_along_axis(table, (jnp.arange(top)[None, :] + rotation) % top, axis=1)


def load_shares(count, total, bound, slope, full):
    loads = [(1 << 20) // math.isqrt(grade ** slope) + 1 for grade in range(1, count + 1)]
    largest = bound if full else min(bound, max(-(-total // count), total * loads[0] // sum(loads)))
    least = 1 if total - largest >= count - 1 else 0
    given, spare = [largest] + [least] * (count - 1), total - largest - least * (count - 1)
    while spare > 0:
        free = [i for i in range(1, count) if given[i] < largest] or [i for i in range(1, count) if given[i] < bound]
        pool, remaining = sum([loads[i] for i in free]), spare
        for i in free:
            extra = min(bound - given[i], max(1, remaining * loads[i] // pool), spare)
            given[i] = given[i] + extra
            spare = spare - extra
    return np.array(given)


def noise(key, shape, spread, reach, split=(), kind=jnp.bfloat16):
    result = spread * jax.random.normal(key, shape, jnp.float32)
    if split:
        result = result * block_levels(key, shape, split, -0.22, 0.18)
    return jnp.clip(result, -reach, reach).astype(kind)


def setup_inputs(seed: int = 0) -> dict:
    splits = jax.random.split(jax.random.key(seed), 8)
    quant_tokens = noise(splits[0], (TOKENS, D), 1.0, 6.0, ((0, 32),))
    token_scales = jnp.clip(jnp.exp(math.log(2.5) - 2.5257286 * jax.random.uniform(splits[1], (TOKENS, NBLK), jnp.float32) ** block_levels(splits[1], (TOKENS, NBLK), ((0, 32),), -0.2, 0.2)), 0.2, 2.5)
    expert_ids_keys = jax.random.split(jax.random.fold_in(splits[2], 1), TOKENS // BLK)
    expert_ids_turns = jax.random.permutation(jax.random.fold_in(splits[2], 3), TOKENS // BLK)
    expert_ids = jax.vmap(lambda own, number: routed_block(jax.random.fold_in(splits[2], 2), own, number, BLK, EXPERTS, TOP, CAP, 2))(expert_ids_keys, expert_ids_turns).reshape((TOKENS, TOP))
    gate_weights = jnp.clip(0.049804688 + 0.9501953 * jax.random.uniform(splits[3], (TOKENS, TOP), jnp.float32) ** block_levels(splits[3], (TOKENS, TOP), ((0, 32),), -0.2, 0.2), 0.049804688, 1.0).astype(jnp.bfloat16)
    grad_out = noise(splits[4], (TOKENS, D), 0.5, 4.0, ((0, 32),))
    w_in = noise(splits[5], (D, EXPERTS, 2, HID), D ** -0.5, 0.078125, ((1, 16), (3, 2)))
    w_out = noise(splits[6], (D, EXPERTS, HID), HID ** -0.5, 0.15625, ((1, 16), (2, 2)))
    return {"quant_tokens": quant_tokens, "token_scales": token_scales, "expert_ids": expert_ids, "gate_weights": gate_weights, "grad_out": grad_out, "w_in": w_in, "w_out": w_out}


def reference(quant_tokens, token_scales, expert_ids, gate_weights, grad_out, w_in, w_out):
    blocks = token_scales.shape[1]
    scaled = (quant_tokens.astype(jnp.float32).reshape(TOKENS, blocks, D // blocks) * token_scales[:, :, None]).reshape(TOKENS, D).astype(jnp.bfloat16)
    most_rows = (TOKENS // BLK) * CAP
    half_length = TOKENS // N_DP
    group_width = HID // N_TENSOR
    zero_half = jnp.zeros((), jnp.bfloat16)

    def per_expert(carry, expert):
        grad_acc, gate_acc = carry
        chosen = expert_ids == expert
        present = jnp.any(chosen, axis=1)
        count = jnp.sum(present.astype(jnp.int32))
        index = jnp.nonzero(present, size=most_rows, fill_value=0)[0].astype(jnp.int32)
        valid = jnp.arange(most_rows, dtype=jnp.int32) < count
        token_gate = jnp.sum(jnp.where(chosen, gate_weights.astype(jnp.float32), 0.0), axis=1)
        gate_rows = jnp.where(valid, token_gate[index], 0.0)
        inputs = jnp.where(valid[:, None], scaled[index], zero_half)
        cotangent = jnp.where(valid[:, None], grad_out[index], zero_half)
        weight_in = lax.dynamic_index_in_dim(w_in, expert, axis=1, keepdims=False).astype(jnp.float32)
        weight_out = lax.dynamic_index_in_dim(w_out, expert, axis=1, keepdims=False).astype(jnp.float32)
        projected = jnp.einsum('rd,djh->rjh', inputs.astype(jnp.float32), weight_in)
        gate_pre = projected[:, 0]
        up_value = projected[:, 1]
        back = jnp.einsum('rd,dh->rh', cotangent.astype(jnp.float32), weight_out)
        sigmoid_gate = jax.nn.sigmoid(gate_pre)
        activated = gate_pre * sigmoid_gate
        hidden = activated * up_value
        gate_piece = (hidden * back).reshape(most_rows, N_TENSOR, group_width).sum(axis=2).astype(jnp.bfloat16)
        gate_sum = jnp.sum(lax.optimization_barrier(gate_piece).astype(jnp.float32), axis=1)
        grad_hidden = gate_rows[:, None] * back
        grad_pre = grad_hidden * up_value * sigmoid_gate * (1.0 + gate_pre * (1.0 - sigmoid_gate))
        grad_up = grad_hidden * activated
        grad_both = jnp.stack([grad_pre, grad_up], axis=1).astype(jnp.bfloat16)
        pieces = jnp.einsum('rjth,djth->trd', grad_both.astype(jnp.float32).reshape(most_rows, 2, N_TENSOR, group_width), weight_in.reshape(D, 2, N_TENSOR, group_width))
        pieces = lax.optimization_barrier(pieces.astype(jnp.bfloat16)).astype(jnp.float32)
        row_grad = jnp.sum(pieces, axis=0)
        scaled_hidden = (gate_rows[:, None] * hidden).astype(jnp.bfloat16)
        owner_half = index // half_length
        total_in = jnp.zeros((D, 2, HID), jnp.float32)
        total_out = jnp.zeros((D, HID), jnp.float32)
        for half in range(N_DP):
            member = valid & (owner_half == half)
            half_inputs = jnp.where(member[:, None], inputs, zero_half).astype(jnp.float32)
            half_cotangent = jnp.where(member[:, None], cotangent, zero_half).astype(jnp.float32)
            half_in = jnp.einsum('rd,rjh->djh', half_inputs, grad_both.astype(jnp.float32)).astype(jnp.bfloat16)
            half_out = jnp.einsum('rd,rh->dh', half_cotangent, scaled_hidden.astype(jnp.float32)).astype(jnp.bfloat16)
            total_in = total_in + lax.optimization_barrier(half_in).astype(jnp.float32)
            total_out = total_out + lax.optimization_barrier(half_out).astype(jnp.float32)
        grad_acc = grad_acc.at[index].add(jnp.where(valid[:, None], row_grad, 0.0))
        gate_terms = jnp.where(chosen[index] & valid[:, None], gate_sum[:, None], 0.0)
        gate_acc = gate_acc.at[index].add(gate_terms)
        return (grad_acc, gate_acc), (total_in.astype(jnp.bfloat16), total_out.astype(jnp.bfloat16))

    start = (jnp.zeros((TOKENS, D), jnp.float32), jnp.zeros((TOKENS, TOP), jnp.float32))
    (grad_acc, gate_acc), (grads_in, grads_out) = lax.scan(per_expert, start, jnp.arange(EXPERTS, dtype=jnp.int32))
    grad_w_in = jnp.transpose(grads_in, (1, 0, 2, 3))
    grad_w_out = jnp.transpose(grads_out, (1, 0, 2))
    return (grad_acc.astype(jnp.bfloat16), gate_acc, grad_w_in, grad_w_out)
```

```python
import jax
import jax.numpy as jnp
from jax import lax
from jax.experimental import pallas as pl
from jax.experimental.pallas import tpu as pltpu
from jax.sharding import PartitionSpec as P

LANES = 128


def slot_table(routes_all, experts, n_expert, capacity):
    block, top = routes_all.shape
    flat_ids = routes_all.reshape(block * top)
    onehot = (flat_ids[:, None] == jnp.arange(experts, dtype=jnp.int32)[None, :]).astype(jnp.int32)
    before = jnp.sum(onehot * (jnp.cumsum(onehot, axis=0) - 1), axis=1)
    held = experts // n_expert
    owner = flat_ids // held
    local_index = flat_ids % held
    slot_of = ((local_index * n_expert + owner) * capacity + before).reshape(block, top)
    return jnp.arange(experts * capacity, dtype=jnp.int32)[:, None, None] == slot_of[None]


def expert_math(projected, back, gate_rows):
    gate_pre = projected[:, :, 0]
    up_value = projected[:, :, 1]
    sigmoid_gate = jax.nn.sigmoid(gate_pre)
    activated = gate_pre * sigmoid_gate
    hidden = activated * up_value
    gate_piece = jnp.sum(hidden * back, axis=2).astype(jnp.bfloat16)
    grad_hidden = gate_rows * back
    grad_pre = grad_hidden * up_value * sigmoid_gate * (1.0 + gate_pre * (1.0 - sigmoid_gate))
    grad_up = grad_hidden * activated
    grad_both = jnp.stack([grad_pre, grad_up], axis=2).astype(jnp.bfloat16)
    scaled_hidden = (gate_rows * hidden).astype(jnp.bfloat16)
    return (gate_piece, grad_both, scaled_hidden)


def routed_body(quant_tokens, token_scales, expert_ids, gate_weights, grad_out, w_in, w_out):
    tok_dev, width = quant_tokens.shape
    blocks = token_scales.shape[1]
    top = expert_ids.shape[1]
    n_tensor = lax.axis_size("tensor")
    n_expert = lax.axis_size("expert")
    held = w_in.shape[1]
    experts = held * n_expert
    block = tok_dev * n_tensor
    capacity = max(2, block * top * 13 // (12 * experts))
    rows = n_expert * capacity
    slots = experts * capacity
    share = width // n_tensor
    hidden_dev = w_out.shape[2]
    scaled = (
        (
            quant_tokens.astype(jnp.float32).reshape(tok_dev, blocks, width // blocks)
            * token_scales[:, :, None]
        )
        .reshape(tok_dev, width)
        .astype(jnp.bfloat16)
    )
    routes_all = lax.all_gather(expert_ids, "tensor", axis=0, tiled=True)
    routed = slot_table(routes_all, experts, n_expert, capacity)
    routed_float = routed.astype(jnp.float32)
    placing = jnp.any(routed, axis=2).astype(jnp.bfloat16)
    gates_all = lax.all_gather(gate_weights, "tensor", axis=0, tiled=True)
    tokens_part, cotangent_part = (
        lax.all_to_all(scaled, "tensor", split_axis=1, concat_axis=0, tiled=True),
        lax.all_to_all(grad_out, "tensor", split_axis=1, concat_axis=0, tiled=True),
    )
    slot_gates = jnp.einsum(
        "stk,tk->s", routed_float, gates_all.astype(jnp.float32), precision=lax.Precision.HIGHEST
    )
    slot_inputs = (
        jnp.dot(placing, tokens_part, preferred_element_type=jnp.float32)
        .astype(jnp.bfloat16)
        .reshape(held, n_expert, capacity, share)
    )
    slot_cotangent = (
        jnp.dot(placing, cotangent_part, preferred_element_type=jnp.float32)
        .astype(jnp.bfloat16)
        .reshape(held, n_expert, capacity, share)
    )
    part_inputs, part_cotangent, recv_gates = (
        lax.all_to_all(slot_inputs, "expert", split_axis=1, concat_axis=1, tiled=True),
        lax.all_to_all(slot_cotangent, "expert", split_axis=1, concat_axis=1, tiled=True),
        lax.all_to_all(
            slot_gates.astype(jnp.bfloat16).reshape(held, n_expert, capacity),
            "expert",
            split_axis=1,
            concat_axis=1,
            tiled=True,
        ),
    )
    recv_inputs, recv_cotangent = (
        lax.all_gather(part_inputs, "tensor", axis=3, tiled=True),
        lax.all_gather(part_cotangent, "tensor", axis=3, tiled=True),
    )
    inputs = recv_inputs.reshape(held, rows, width)
    cotangent = recv_cotangent.reshape(held, rows, width)
    gate_flat = recv_gates.reshape(held, rows).astype(jnp.float32)
    weights_in_all, weights_out_all = (
        lax.all_gather(w_in, "dp", axis=0, tiled=True),
        lax.all_gather(w_out, "dp", axis=0, tiled=True),
    )
    projected = jnp.einsum(
        "erd,dejh->erjh", inputs, weights_in_all, preferred_element_type=jnp.float32
    )
    back = jnp.einsum(
        "erd,deh->erh", cotangent, weights_out_all, preferred_element_type=jnp.float32
    )
    gate_piece, grad_both, scaled_hidden = expert_math(projected, back, gate_flat[:, :, None])
    token_piece = jnp.einsum(
        "erjh,dejh->erd", grad_both, weights_in_all, preferred_element_type=jnp.float32
    ).astype(jnp.bfloat16)
    term_in = jnp.einsum(
        "erd,erjh->dejh", inputs, grad_both, preferred_element_type=jnp.float32
    ).reshape(w_in.shape[0] * lax.axis_size("dp"), held, 2 * hidden_dev)
    term_out = jnp.einsum(
        "erd,erh->deh", cotangent, scaled_hidden, preferred_element_type=jnp.float32
    )
    summed = lax.psum_scatter(
        jnp.concatenate([term_in, term_out], axis=2).astype(jnp.bfloat16),
        "dp",
        scatter_dimension=0,
        tiled=True,
    ).astype(jnp.float32)
    grad_w_in = (
        summed[:, :, : 2 * hidden_dev]
        .astype(jnp.bfloat16)
        .reshape(w_in.shape[0], held, 2, hidden_dev)
    )
    grad_w_out = summed[:, :, 2 * hidden_dev :].astype(jnp.bfloat16)
    piece_float = (
        lax.optimization_barrier(token_piece)
        .astype(jnp.float32)
        .reshape(held, n_expert, capacity, width)
    )
    gate_float = (
        lax.optimization_barrier(gate_piece).astype(jnp.float32).reshape(held, n_expert, capacity)
    )
    slot_total = lax.psum_scatter(
        piece_float.astype(jnp.bfloat16), "tensor", scatter_dimension=3, tiled=True
    ).astype(jnp.float32)
    gate_total = lax.psum(gate_float, "tensor")
    back_cols, back_gates = (
        lax.all_to_all(
            slot_total.astype(jnp.bfloat16), "expert", split_axis=1, concat_axis=1, tiled=True
        ).astype(slot_total.dtype),
        lax.all_to_all(
            gate_total.astype(jnp.bfloat16), "expert", split_axis=1, concat_axis=1, tiled=True
        ).astype(gate_total.dtype),
    )
    token_cols_all = jnp.einsum(
        "st,sd->td",
        placing.astype(jnp.float32),
        back_cols.reshape(slots, share),
        precision=lax.Precision.HIGHEST,
    ).astype(jnp.bfloat16)
    grad_tokens = lax.all_to_all(token_cols_all, "tensor", split_axis=0, concat_axis=1, tiled=True)
    token_gate = jnp.einsum(
        "stk,s->tk", routed_float, back_gates.reshape(slots), precision=lax.Precision.HIGHEST
    )
    mine_gate = lax.dynamic_slice_in_dim(token_gate, lax.axis_index("tensor") * tok_dev, tok_dev, 0)
    return (grad_tokens, mine_gate, grad_w_in, grad_w_out)


def swap(array, stage):
    axis, bit = stage
    size = lax.axis_size(axis)
    return lax.ppermute(array, axis, [(i, i ^ bit) for i in range(size)])


def doubling_gather(rows, order):
    for stage in order:
        rows = jnp.concatenate([rows, swap(rows, stage)], axis=0)
    return rows


def halving_sum(total, order):
    for stage in order:
        half = total.shape[0] // 2
        sent = swap(total[half:].astype(jnp.bfloat16), stage)
        total = total[:half] + sent.astype(jnp.float32)
    return total


def order_matrix(order, base, tok_dev):
    count = tok_dev << len(order)
    position = lax.broadcasted_iota(jnp.int32, (count, count), 1)
    block, offset = position // tok_dev, position % tok_dev
    target = jnp.zeros_like(block)
    for place, stage in enumerate(order):
        target = target + ((block >> place) & 1) * (1 << base.index(stage))
    source = lax.broadcasted_iota(jnp.int32, (count, count), 0)
    return (source == target * tok_dev + offset).astype(jnp.bfloat16)


def weight_grad_kernel(inputs, cotangent, gate_grad, up_grad, scaled, *rest):
    grad_in, grad_out = rest[-2:]
    contract = (((0,), (0,)), ((), ()))
    x, g = inputs[...], cotangent[...]
    grad_in[:, 0, :] = lax.dot_general(
        x, gate_grad[...], contract, preferred_element_type=jnp.float32
    ).astype(jnp.bfloat16)
    grad_in[:, 1, :] = lax.dot_general(
        x, up_grad[...], contract, preferred_element_type=jnp.float32
    ).astype(jnp.bfloat16)
    grad_out[...] = lax.dot_general(
        g, scaled[...], contract, preferred_element_type=jnp.float32
    ).astype(jnp.bfloat16)


def weight_grads(inputs, cotangent, gate_grad, up_grad, scaled, start, width, so_far):
    rows, columns = inputs.shape
    hidden = gate_grad.shape[1]
    tile = 512 if columns % 512 == 0 else columns
    first = start // tile
    resident = pl.BlockSpec((rows, hidden), lambda i: (0, 0))
    stream = pl.BlockSpec((rows, tile), lambda i: (0, i))
    kept = [pl.BlockSpec(memory_space=pl.ANY)] * len(so_far)
    return pl.pallas_call(
        weight_grad_kernel,
        grid=(columns // tile,),
        in_specs=[stream, stream, resident, resident, resident] + kept,
        out_specs=[
            pl.BlockSpec((tile, 2, hidden), lambda i: (first + i, 0, 0)),
            pl.BlockSpec((tile, hidden), lambda i: (first + i, 0)),
        ],
        out_shape=[
            jax.ShapeDtypeStruct((width, 2, hidden), jnp.bfloat16),
            jax.ShapeDtypeStruct((width, hidden), jnp.bfloat16),
        ],
        input_output_aliases={5: 0, 6: 1} if so_far else {},
        compiler_params=pltpu.CompilerParams(vmem_limit_bytes=24 << 20),
        cost_estimate=pl.CostEstimate(
            flops=6 * rows * columns * hidden,
            bytes_accessed=6 * columns * hidden + 4 * rows * columns,
            transcendentals=0,
        ),
    )(inputs, cotangent, gate_grad, up_grad, scaled, *so_far)


def gathered_body(quant_tokens, token_scales, expert_ids, gate_weights, grad_out, w_in, w_out):
    tok_dev, width = quant_tokens.shape
    blocks = token_scales.shape[1]
    top = expert_ids.shape[1]
    n_tensor = lax.axis_size("tensor")
    n_expert = lax.axis_size("expert")
    tokens = tok_dev * n_tensor * n_expert
    capacity = max(2, tok_dev * n_tensor * top * 13 // (12 * n_expert))
    slots = n_expert * capacity
    hidden = w_out.shape[2]
    expert = lax.axis_index("expert")

    core, across = [("expert", 1)], [("expert", 2)]
    along = [("expert", 1 << k) for k in range(2, n_expert.bit_length() - 1)][::-1]
    side = [("tensor", 1 << k) for k in range(n_tensor.bit_length() - 1)]
    orders = [
        side + along + across + core,
        along + across + side + core,
        along + side + across + core,
        along + across + side + core,
        across + side + along + core,
    ]
    base = orders[0]
    chunk = width // len(orders)

    scaled = (
        (
            quant_tokens.astype(jnp.float32).reshape(tok_dev, blocks, width // blocks)
            * token_scales[:, :, None]
        )
        .reshape(tok_dev, width)
        .astype(jnp.bfloat16)
    )
    routes = jnp.concatenate([expert_ids.astype(jnp.bfloat16), gate_weights], axis=1)
    routes = jnp.pad(routes, ((0, 0), (0, LANES - 2 * top)))

    gathered = []
    for index, order in enumerate(orders):
        lo, hi = index * chunk, (index + 1) * chunk
        parts = [scaled[:, lo:hi], grad_out[:, lo:hi]] + ([routes] if index == 0 else [])
        gathered.append(doubling_gather(jnp.concatenate(parts, axis=1), order))

    routes_all = gathered[0][:, 2 * chunk :].astype(jnp.float32)
    lane = lax.broadcasted_iota(jnp.int32, routes_all.shape, 1)
    named = (routes_all == expert.astype(jnp.float32)) & (lane < top)
    chosen = jnp.any(named, axis=1, keepdims=True)
    gate_lanes = jnp.pad(routes_all[:, top:], ((0, 0), (0, top)))
    token_gate = jnp.sum(jnp.where(named, gate_lanes, 0.0), axis=1, keepdims=True)
    earlier = lax.broadcasted_iota(jnp.int32, (tokens, tokens), 0)
    later = lax.broadcasted_iota(jnp.int32, (tokens, tokens), 1)
    far = 2 * tokens
    ranking = jnp.where(earlier == later, -far, (earlier < later).astype(jnp.int32))
    rank = far + lax.dot_general(
        chosen.astype(jnp.bfloat16),
        ranking.astype(jnp.bfloat16),
        (((0,), (0,)), ((), ())),
        preferred_element_type=jnp.float32,
    )
    slot = lax.broadcasted_iota(jnp.int32, (slots, tokens), 0).astype(jnp.float32)
    placing = (slot == rank).astype(jnp.bfloat16)
    slot_gates = jnp.dot(
        placing, token_gate.astype(jnp.bfloat16), preferred_element_type=jnp.float32
    )
    placings = {}
    for order in orders:
        key = tuple(order)
        if key not in placings:
            placings[key] = (
                placing
                if order == base
                else jnp.dot(
                    placing,
                    order_matrix(order, base, tok_dev),
                    preferred_element_type=jnp.float32,
                ).astype(jnp.bfloat16)
            )

    gate_pre = up_value = back = None
    inputs, cotangents = [], []
    for index, order in enumerate(orders):
        lo, hi = index * chunk, (index + 1) * chunk
        picked = jnp.dot(
            placings[tuple(order)],
            gathered[index][:, : 2 * chunk],
            preferred_element_type=jnp.float32,
        ).astype(jnp.bfloat16)
        x, g = picked[:, :chunk], picked[:, chunk:]
        inputs.append(x)
        cotangents.append(g)
        part = jnp.einsum("rd,djh->rjh", x, w_in[lo:hi, 0], preferred_element_type=jnp.float32)
        back_part = jnp.dot(g, w_out[lo:hi, 0], preferred_element_type=jnp.float32)
        projected = part if index == 0 else projected + part
        back = back_part if index == 0 else back + back_part
    gate_pre, up_value = projected[:, 0], projected[:, 1]
    sigmoid_gate = jax.nn.sigmoid(gate_pre)
    activated = gate_pre * sigmoid_gate
    hidden_value = activated * up_value
    gate_piece = jnp.sum(hidden_value * back, axis=1, keepdims=True).astype(jnp.bfloat16)
    grad_hidden = slot_gates * back
    gate_grad = (
        grad_hidden * up_value * sigmoid_gate * (1.0 + gate_pre * (1.0 - sigmoid_gate))
    ).astype(jnp.bfloat16)
    up_grad = (grad_hidden * activated).astype(jnp.bfloat16)
    scaled_hidden = (slot_gates * hidden_value).astype(jnp.bfloat16)
    grad_both = jnp.stack([gate_grad, up_grad], axis=1)

    summed = []
    transposed = (((0,), (0,)), ((), ()))
    for index, order in enumerate(orders):
        lo, hi = index * chunk, (index + 1) * chunk
        piece = jnp.einsum(
            "rjh,djh->rd", grad_both, w_in[lo:hi, 0], preferred_element_type=jnp.float32
        ).astype(jnp.bfloat16)
        total = lax.dot_general(
            placings[tuple(order)], piece, transposed, preferred_element_type=jnp.float32
        )
        if index == 0:
            token_piece = lax.dot_general(
                placing, gate_piece, transposed, preferred_element_type=jnp.float32
            )
            total = jnp.concatenate([total, jnp.where(named, token_piece, 0.0)], axis=1)
        summed.append(halving_sum(total, order[::-1]))
    grad_gates = summed[0][:, chunk : chunk + top]
    summed[0] = summed[0][:, :chunk]
    grad_tokens = jnp.concatenate([s.astype(jnp.bfloat16) for s in summed], axis=1)

    grads = ()
    for index in range(len(orders)):
        grads = weight_grads(
            inputs[index],
            cotangents[index],
            gate_grad,
            up_grad,
            scaled_hidden,
            index * chunk,
            width,
            grads,
        )
    return (
        grad_tokens,
        grad_gates,
        grads[0].reshape(width, 1, 2, hidden),
        grads[1].reshape(width, 1, hidden),
    )


def body(*arrays):
    quant_tokens, w_in = arrays[0], arrays[5]
    sizes = [lax.axis_size(name) for name in ("expert", "tensor")]
    whole = lax.axis_size("dp") == 1 and w_in.shape[1] == 1
    doubling = all(size & (size - 1) == 0 for size in sizes) and sizes[0] >= 4
    few = quant_tokens.shape[0] * sizes[0] * sizes[1] <= 1024
    tiled = quant_tokens.shape[1] % (5 * 512) == 0
    chosen = gathered_body if whole and doubling and few and tiled else routed_body
    return chosen(*arrays)


def solution(mesh):
    in_specs = (
        P(("dp", "expert", "tensor"), None),
        P(("dp", "expert", "tensor"), None),
        P(("dp", "expert", "tensor"), None),
        P(("dp", "expert", "tensor"), None),
        P(("dp", "expert", "tensor"), None),
        P("dp", "expert", None, "tensor"),
        P("dp", "expert", "tensor"),
    )
    out_specs = (
        P(("dp", "expert", "tensor"), None),
        P(("dp", "expert", "tensor"), None),
        P("dp", "expert", None, "tensor"),
        P("dp", "expert", "tensor"),
    )
    return jax.shard_map(body, mesh=mesh, in_specs=in_specs, out_specs=out_specs, check_vma=False)
```

```python
import jax
import jax.numpy as jnp
from jax import lax
from jax.experimental import pallas as pl
from jax.experimental.pallas import tpu as pltpu
from jax.sharding import PartitionSpec as P

LANES = 128
FIRST = (((0,), (0,)), ((), ()))
LAST = (((1,), (1,)), ((), ()))


def slot_table(routes_all, experts, n_expert, capacity):
    block, top = routes_all.shape
    flat_ids = routes_all.reshape(block * top)
    onehot = (flat_ids[:, None] == jnp.arange(experts, dtype=jnp.int32)[None, :]).astype(jnp.int32)
    before = jnp.sum(onehot * (jnp.cumsum(onehot, axis=0) - 1), axis=1)
    held = experts // n_expert
    owner = flat_ids // held
    local_index = flat_ids % held
    slot_of = ((local_index * n_expert + owner) * capacity + before).reshape(block, top)
    return jnp.arange(experts * capacity, dtype=jnp.int32)[:, None, None] == slot_of[None]


def expert_math(projected, back, gate_rows):
    gate_pre = projected[:, :, 0]
    up_value = projected[:, :, 1]
    sigmoid_gate = jax.nn.sigmoid(gate_pre)
    activated = gate_pre * sigmoid_gate
    hidden = activated * up_value
    gate_piece = jnp.sum(hidden * back, axis=2).astype(jnp.bfloat16)
    grad_hidden = gate_rows * back
    grad_pre = grad_hidden * up_value * sigmoid_gate * (1.0 + gate_pre * (1.0 - sigmoid_gate))
    grad_up = grad_hidden * activated
    grad_both = jnp.stack([grad_pre, grad_up], axis=2).astype(jnp.bfloat16)
    scaled_hidden = (gate_rows * hidden).astype(jnp.bfloat16)
    return (gate_piece, grad_both, scaled_hidden)


def routed_body(quant_tokens, token_scales, expert_ids, gate_weights, grad_out, w_in, w_out):
    tok_dev, width = quant_tokens.shape
    blocks = token_scales.shape[1]
    top = expert_ids.shape[1]
    n_tensor = lax.axis_size("tensor")
    n_expert = lax.axis_size("expert")
    held = w_in.shape[1]
    experts = held * n_expert
    block = tok_dev * n_tensor
    capacity = max(2, block * top * 13 // (12 * experts))
    rows = n_expert * capacity
    slots = experts * capacity
    share = width // n_tensor
    hidden_dev = w_out.shape[2]
    scaled = (
        (
            quant_tokens.astype(jnp.float32).reshape(tok_dev, blocks, width // blocks)
            * token_scales[:, :, None]
        )
        .reshape(tok_dev, width)
        .astype(jnp.bfloat16)
    )
    routes_all = lax.all_gather(expert_ids, "tensor", axis=0, tiled=True)
    routed = slot_table(routes_all, experts, n_expert, capacity)
    routed_float = routed.astype(jnp.float32)
    placing = jnp.any(routed, axis=2).astype(jnp.bfloat16)
    gates_all = lax.all_gather(gate_weights, "tensor", axis=0, tiled=True)
    tokens_part, cotangent_part = (
        lax.all_to_all(scaled, "tensor", split_axis=1, concat_axis=0, tiled=True),
        lax.all_to_all(grad_out, "tensor", split_axis=1, concat_axis=0, tiled=True),
    )
    slot_gates = jnp.einsum(
        "stk,tk->s", routed_float, gates_all.astype(jnp.float32), precision=lax.Precision.HIGHEST
    )
    slot_inputs = (
        jnp.dot(placing, tokens_part, preferred_element_type=jnp.float32)
        .astype(jnp.bfloat16)
        .reshape(held, n_expert, capacity, share)
    )
    slot_cotangent = (
        jnp.dot(placing, cotangent_part, preferred_element_type=jnp.float32)
        .astype(jnp.bfloat16)
        .reshape(held, n_expert, capacity, share)
    )
    part_inputs, part_cotangent, recv_gates = (
        lax.all_to_all(slot_inputs, "expert", split_axis=1, concat_axis=1, tiled=True),
        lax.all_to_all(slot_cotangent, "expert", split_axis=1, concat_axis=1, tiled=True),
        lax.all_to_all(
            slot_gates.astype(jnp.bfloat16).reshape(held, n_expert, capacity),
            "expert",
            split_axis=1,
            concat_axis=1,
            tiled=True,
        ),
    )
    recv_inputs, recv_cotangent = (
        lax.all_gather(part_inputs, "tensor", axis=3, tiled=True),
        lax.all_gather(part_cotangent, "tensor", axis=3, tiled=True),
    )
    inputs = recv_inputs.reshape(held, rows, width)
    cotangent = recv_cotangent.reshape(held, rows, width)
    gate_flat = recv_gates.reshape(held, rows).astype(jnp.float32)
    weights_in_all, weights_out_all = (
        lax.all_gather(w_in, "dp", axis=0, tiled=True),
        lax.all_gather(w_out, "dp", axis=0, tiled=True),
    )
    projected = jnp.einsum(
        "erd,dejh->erjh", inputs, weights_in_all, preferred_element_type=jnp.float32
    )
    back = jnp.einsum(
        "erd,deh->erh", cotangent, weights_out_all, preferred_element_type=jnp.float32
    )
    gate_piece, grad_both, scaled_hidden = expert_math(projected, back, gate_flat[:, :, None])
    token_piece = jnp.einsum(
        "erjh,dejh->erd", grad_both, weights_in_all, preferred_element_type=jnp.float32
    ).astype(jnp.bfloat16)
    term_in = jnp.einsum(
        "erd,erjh->dejh", inputs, grad_both, preferred_element_type=jnp.float32
    ).reshape(w_in.shape[0] * lax.axis_size("dp"), held, 2 * hidden_dev)
    term_out = jnp.einsum(
        "erd,erh->deh", cotangent, scaled_hidden, preferred_element_type=jnp.float32
    )
    summed = lax.psum_scatter(
        jnp.concatenate([term_in, term_out], axis=2).astype(jnp.bfloat16),
        "dp",
        scatter_dimension=0,
        tiled=True,
    ).astype(jnp.float32)
    grad_w_in = (
        summed[:, :, : 2 * hidden_dev]
        .astype(jnp.bfloat16)
        .reshape(w_in.shape[0], held, 2, hidden_dev)
    )
    grad_w_out = summed[:, :, 2 * hidden_dev :].astype(jnp.bfloat16)
    piece_float = (
        lax.optimization_barrier(token_piece)
        .astype(jnp.float32)
        .reshape(held, n_expert, capacity, width)
    )
    gate_float = (
        lax.optimization_barrier(gate_piece).astype(jnp.float32).reshape(held, n_expert, capacity)
    )
    slot_total = lax.psum_scatter(
        piece_float.astype(jnp.bfloat16), "tensor", scatter_dimension=3, tiled=True
    ).astype(jnp.float32)
    gate_total = lax.psum(gate_float, "tensor")
    back_cols, back_gates = (
        lax.all_to_all(
            slot_total.astype(jnp.bfloat16), "expert", split_axis=1, concat_axis=1, tiled=True
        ).astype(slot_total.dtype),
        lax.all_to_all(
            gate_total.astype(jnp.bfloat16), "expert", split_axis=1, concat_axis=1, tiled=True
        ).astype(gate_total.dtype),
    )
    token_cols_all = jnp.einsum(
        "st,sd->td",
        placing.astype(jnp.float32),
        back_cols.reshape(slots, share),
        precision=lax.Precision.HIGHEST,
    ).astype(jnp.bfloat16)
    grad_tokens = lax.all_to_all(token_cols_all, "tensor", split_axis=0, concat_axis=1, tiled=True)
    token_gate = jnp.einsum(
        "stk,s->tk", routed_float, back_gates.reshape(slots), precision=lax.Precision.HIGHEST
    )
    mine_gate = lax.dynamic_slice_in_dim(token_gate, lax.axis_index("tensor") * tok_dev, tok_dev, 0)
    return (grad_tokens, mine_gate, grad_w_in, grad_w_out)


def after(value, *others):
    return lax.optimization_barrier((value,) + others)[0]


def swap(array, stage):
    n_expert, n_tensor = lax.axis_size("expert"), lax.axis_size("tensor")
    pairs = []
    for e in range(n_expert):
        for t in range(n_tensor):
            axis, bit = stage[e & 1]
            e_to, t_to = (e ^ bit, t) if axis == "expert" else (e, t ^ bit)
            pairs.append((e * n_tensor + t, e_to * n_tensor + t_to))
    return lax.ppermute(array, ("expert", "tensor"), pairs)


def order_matrix(order, base, tok_dev):
    count = tok_dev << len(order)
    position = lax.broadcasted_iota(jnp.int32, (count, count), 1)
    block, offset = position // tok_dev, position % tok_dev
    top = len(order) - 1
    half = block >> top
    targets = []
    for core in range(2):
        where = [stage[core] for stage in base]
        target = half << top
        for place in range(top):
            bit = (block >> place) & 1
            target = target + (bit << where.index(order[place][core]))
        targets.append(target)
    owner = half ^ (lax.axis_index("expert") & 1)
    target = jnp.where(owner == 0, targets[0], targets[1])
    source = lax.broadcasted_iota(jnp.int32, (count, count), 0)
    return (source == target * tok_dev + offset).astype(jnp.bfloat16)


def pick_kernel(place, *refs):
    blocks, out = refs[:4], refs[-1]
    rows = jnp.concatenate([block[...] for block in blocks], axis=0)
    out[...] = jnp.dot(place[...], rows, preferred_element_type=jnp.float32).astype(jnp.bfloat16)


def pick(place, blocks, columns, start, width, so_far):
    slots, tokens = place.shape
    tile = 512
    first = start // tile
    kept = [pl.BlockSpec(memory_space=pl.ANY)] * len(so_far)
    return pl.pallas_call(
        pick_kernel,
        grid=(columns // tile,),
        in_specs=[pl.BlockSpec((slots, tokens), lambda i: (0, 0))]
        + [pl.BlockSpec((tokens // 4, tile), lambda i: (0, i))] * 4
        + kept,
        out_specs=pl.BlockSpec((slots, tile), lambda i: (0, first + i)),
        out_shape=jax.ShapeDtypeStruct((slots, width), jnp.bfloat16),
        input_output_aliases={5: 0} if so_far else {},
        compiler_params=pltpu.CompilerParams(vmem_limit_bytes=16 << 20),
        cost_estimate=pl.CostEstimate(
            flops=2 * slots * columns * tokens,
            bytes_accessed=2 * columns * (tokens + slots),
            transcendentals=0,
        ),
    )(place, *blocks, *so_far)


def weight_grad_kernel(inputs, cotangent, gate_grad, up_grad, scaled, *rest):
    grad_in, grad_out = rest[-2:]
    x, g = inputs[...], cotangent[...]
    grad_in[:, 0, :] = lax.dot_general(
        x, gate_grad[...], FIRST, preferred_element_type=jnp.float32
    ).astype(jnp.bfloat16)
    grad_in[:, 1, :] = lax.dot_general(
        x, up_grad[...], FIRST, preferred_element_type=jnp.float32
    ).astype(jnp.bfloat16)
    grad_out[...] = lax.dot_general(
        g, scaled[...], FIRST, preferred_element_type=jnp.float32
    ).astype(jnp.bfloat16)


def weight_grads(inputs, cotangent, gate_grad, up_grad, scaled, start, columns, so_far):
    rows, hidden = gate_grad.shape
    width = inputs.shape[1]
    tile = 512
    first = start // tile
    resident = pl.BlockSpec((rows, hidden), lambda i: (0, 0))
    stream = pl.BlockSpec((rows, tile), lambda i: (0, first + i))
    kept = [pl.BlockSpec(memory_space=pl.ANY)] * len(so_far)
    return pl.pallas_call(
        weight_grad_kernel,
        grid=(columns // tile,),
        in_specs=[stream, stream, resident, resident, resident] + kept,
        out_specs=[
            pl.BlockSpec((tile, 2, hidden), lambda i: (first + i, 0, 0)),
            pl.BlockSpec((tile, hidden), lambda i: (first + i, 0)),
        ],
        out_shape=[
            jax.ShapeDtypeStruct((width, 2, hidden), jnp.bfloat16),
            jax.ShapeDtypeStruct((width, hidden), jnp.bfloat16),
        ],
        input_output_aliases={5: 0, 6: 1} if so_far else {},
        compiler_params=pltpu.CompilerParams(vmem_limit_bytes=20 << 20),
        cost_estimate=pl.CostEstimate(
            flops=6 * rows * columns * hidden,
            bytes_accessed=6 * columns * hidden + 4 * rows * columns,
            transcendentals=0,
        ),
    )(inputs, cotangent, gate_grad, up_grad, scaled, *so_far)


def gathered_body(quant_tokens, token_scales, expert_ids, gate_weights, grad_out, w_in, w_out):
    tok_dev, width = quant_tokens.shape
    blocks = token_scales.shape[1]
    top = expert_ids.shape[1]
    n_tensor = lax.axis_size("tensor")
    n_expert = lax.axis_size("expert")
    tokens = tok_dev * n_tensor * n_expert
    half = tokens // 2
    capacity = max(2, tok_dev * n_tensor * top * 13 // (12 * n_expert))
    slots = n_expert * capacity
    hidden = w_out.shape[2]
    expert = lax.axis_index("expert")

    both = lambda *stages: [(s, s) for s in stages]
    core, across = ("expert", 1), ("expert", 2)
    along = both(*[("expert", 1 << k) for k in range(2, n_expert.bit_length() - 1)][::-1])
    sides = [("tensor", 1 << k) for k in range(n_tensor.bit_length() - 1)]
    one, two = sides + [across], [across] + sides
    crossed = list(zip(one, two))
    turned = list(zip(two, one))
    last = both(core)
    late = along + crossed + last
    early = turned + along + last
    mid = along[:1] + turned + along[1:] + last
    orders = dict(p=late, d=early, q=late, r=mid, s=late)
    unit = width // 10
    sizes = dict(p=6 * unit, d=4 * unit, q=10 * unit)
    starts = dict(p=0, d=6 * unit, q=0)
    spans = dict(r=(0, 5 * unit), s=(5 * unit, 10 * unit))
    base = orders["p"]

    scaled = (
        (
            quant_tokens.astype(jnp.float32).reshape(tok_dev, blocks, width // blocks)
            * token_scales[:, :, None]
        )
        .reshape(tok_dev, width)
        .astype(jnp.bfloat16)
    )
    routes = jnp.concatenate([expert_ids.astype(jnp.bfloat16), gate_weights], axis=1)
    routes = jnp.pad(routes, ((0, 0), (0, LANES - 2 * top)))

    rows = {}
    for name in "pdq":
        lo, hi = starts[name], starts[name] + sizes[name]
        part = scaled[:, lo:hi] if name in "pd" else grad_out[:, lo:hi]
        rows[name] = jnp.concatenate([part, routes], axis=1) if name == "p" else part

    tips = {}

    def step(name, *others):
        level = (rows[name].shape[0] // tok_dev).bit_length() - 1
        sent = after(rows[name], *others) if others else rows[name]
        got = swap(sent, orders[name][level])
        tips[name] = sent
        rows[name] = jnp.concatenate([sent, got], axis=0) if level < 3 else (sent, got)
        return got

    def finish(name, *others):
        low, high = rows[name]
        far_low = swap(after(low, *others[:-1]) if others[:-1] else low, last[0])
        far_high = swap(after(high, *others[-1:]) if others else high, last[0])
        rows[name] = (low, high, far_low, far_high)
        return far_high

    def make_routes():
        routes_all = jnp.concatenate([r[:, sizes["p"] :] for r in rows["p"]], axis=0)
        routes_all = routes_all.astype(jnp.float32)
        lane = lax.broadcasted_iota(jnp.int32, routes_all.shape, 1)
        named = (routes_all == expert.astype(jnp.float32)) & (lane < top)
        chosen = jnp.any(named, axis=1, keepdims=True)
        gate_lanes = jnp.pad(routes_all[:, top:], ((0, 0), (0, top)))
        token_gate = jnp.sum(jnp.where(named, gate_lanes, 0.0), axis=1, keepdims=True)
        earlier = lax.broadcasted_iota(jnp.int32, (tokens, tokens), 0)
        later = lax.broadcasted_iota(jnp.int32, (tokens, tokens), 1)
        far = 2 * tokens
        ranking = jnp.where(earlier == later, -far, (earlier < later).astype(jnp.int32))
        ranking = ranking.astype(jnp.bfloat16)
        member = chosen.astype(jnp.bfloat16)
        rank = far + lax.dot_general(member, ranking, FIRST, preferred_element_type=jnp.float32)
        slot = lax.broadcasted_iota(jnp.int32, (slots, tokens), 0).astype(jnp.float32)
        placing = (slot == rank).astype(jnp.bfloat16)
        slot_gates = jnp.dot(
            placing, token_gate.astype(jnp.bfloat16), preferred_element_type=jnp.float32
        )
        placings = {}
        for name in orders:
            if orders[name] == base:
                placings[name] = placing
                continue
            moved = order_matrix(orders[name], base, tok_dev)
            placings[name] = jnp.dot(
                placing, moved, preferred_element_type=jnp.float32
            ).astype(jnp.bfloat16)
        return named, slot_gates, placings

    picked = dict(x=(), g=())

    def pick_step(name, *others):
        kind = "x" if name in "pd" else "g"
        place = after(placings[name], *others) if others else placings[name]
        picked[kind] = (
            pick(place, rows[name], sizes[name], starts[name], width, picked[kind]),
        )
        return picked[kind][0]

    p0 = step("p")
    q0 = step("q")
    d0 = step("d")
    halves = {}
    halves["r"] = lax.optimization_barrier(after(w_in, p0)[: 5 * unit, 0])
    halves["s"] = lax.optimization_barrier(after(w_in, q0)[5 * unit :, 0])
    p1 = step("p")
    d1 = step("d", p0)
    d2 = step("d")
    q1 = step("q", p1)
    p2 = step("p")
    p3 = step("p")
    d3 = step("d", p2)
    q2 = step("q", d2)
    finish("p")
    named, slot_gates, placings = make_routes()
    pick_step("p")
    q3 = step("q", d3)
    finish("d")
    inputs = pick_step("d", tips["q"])
    projected = 0.0
    for name in "rs":
        lo, hi = spans[name]
        projected += jnp.einsum(
            "rd,djh->rjh", inputs[:, lo:hi], halves[name], preferred_element_type=jnp.float32
        )
    gate_pre, up_value = projected[:, 0], projected[:, 1]
    finish("q", tips["q"], projected)
    cotangent = pick_step("q")
    back = jnp.dot(cotangent, w_out[:, 0], preferred_element_type=jnp.float32)

    sigmoid_gate = jax.nn.sigmoid(gate_pre)
    activated = gate_pre * sigmoid_gate
    hidden_value = activated * up_value
    gate_piece = jnp.sum(hidden_value * back, axis=1, keepdims=True).astype(jnp.bfloat16)
    grad_hidden = slot_gates * back
    gate_grad = (
        grad_hidden * up_value * sigmoid_gate * (1.0 + gate_pre * (1.0 - sigmoid_gate))
    ).astype(jnp.bfloat16)
    up_grad = (grad_hidden * activated).astype(jnp.bfloat16)
    scaled_hidden = (slot_gates * hidden_value).astype(jnp.bfloat16)

    grads = ()
    sums = {}

    def grad_step(low, high, *others):
        nonlocal grads
        left = after(gate_grad, *others) if others else gate_grad
        grads = weight_grads(
            inputs, cotangent, left, up_grad, scaled_hidden, low, high - low, grads
        )
        return grads[1]

    grad_both = jnp.stack([gate_grad, up_grad], axis=1)

    def piece_step(name, *others):
        lo, hi = spans[name]
        place = placings[name]
        left = after(grad_both, *others) if others else grad_both
        part = jnp.einsum(
            "rjh,djh->rd", left, halves[name], preferred_element_type=jnp.float32
        ).astype(jnp.bfloat16)
        put = lambda rows, kind: lax.dot_general(
            rows, part, FIRST, preferred_element_type=jnp.float32
        ).astype(kind)
        keep, send = put(place[:, :half], jnp.float32), put(place[:, half:], jnp.bfloat16)
        if name == "s":
            token_piece = lax.dot_general(
                place, gate_piece, FIRST, preferred_element_type=jnp.float32
            )
            extra = jnp.where(named, token_piece, 0.0)
            send = jnp.concatenate([send, extra[half:].astype(jnp.bfloat16)], axis=1)
            sums[name] = ([keep, extra[:half]], send)
        else:
            sums[name] = ([keep], send)
        return send

    def sum_step(name, *others):
        keeps, send = sums[name]
        level = (send.shape[0] // tok_dev).bit_length() - 1
        send = after(send, *others) if others else send
        got = swap(send, orders[name][level])
        count = send.shape[0] // 2
        at, new, out = 0, [], []
        for keep in keeps:
            total = keep + got[:, at : at + keep.shape[1]].astype(jnp.float32)
            at += keep.shape[1]
            new.append(total[:count] if level else total)
            out.append(total[count:].astype(jnp.bfloat16))
        send = (out[0] if len(out) == 1 else jnp.concatenate(out, axis=1)) if level else got
        sums[name] = (new, send)
        return send

    sr = piece_step("r")
    r4 = sum_step("r")
    ss = piece_step("s", sr)
    s4 = sum_step("s")
    r3 = sum_step("r", ss)
    s3 = sum_step("s", r4)
    g = grad_step(0, 4 * unit, s4)
    s2 = sum_step("s", g)
    r2 = sum_step("r", s3)
    g = grad_step(4 * unit, 6 * unit, r3)
    s1 = sum_step("s", g)
    r1 = sum_step("r", s2)
    g = grad_step(6 * unit, 8 * unit, r2)
    s0 = sum_step("s", g)
    r0 = sum_step("r", s1)
    g = grad_step(8 * unit, 10 * unit, r1)

    grad_gates = sums["s"][0][1][:, :top]
    grad_tokens = jnp.concatenate([sums[n][0][0].astype(jnp.bfloat16) for n in "rs"], axis=1)
    return (
        grad_tokens,
        grad_gates,
        grads[0].reshape(width, 1, 2, hidden),
        grads[1].reshape(width, 1, hidden),
    )


def body(*arrays):
    quant_tokens, w_in = arrays[0], arrays[5]
    n_expert, n_tensor = lax.axis_size("expert"), lax.axis_size("tensor")
    whole = lax.axis_size("dp") == 1 and w_in.shape[1] == 1
    doubling = n_tensor == 2 and n_expert >= 8 and n_expert & (n_expert - 1) == 0
    few = quant_tokens.shape[0] * n_expert * n_tensor <= 1024
    tiled = quant_tokens.shape[1] % (10 * 512) == 0
    chosen = gathered_body if whole and doubling and few and tiled else routed_body
    return chosen(*arrays)


def solution(mesh):
    in_specs = (
        P(("dp", "expert", "tensor"), None),
        P(("dp", "expert", "tensor"), None),
        P(("dp", "expert", "tensor"), None),
        P(("dp", "expert", "tensor"), None),
        P(("dp", "expert", "tensor"), None),
        P("dp", "expert", None, "tensor"),
        P("dp", "expert", "tensor"),
    )
    out_specs = (
        P(("dp", "expert", "tensor"), None),
        P(("dp", "expert", "tensor"), None),
        P("dp", "expert", None, "tensor"),
        P("dp", "expert", "tensor"),
    )
    return jax.shard_map(body, mesh=mesh, in_specs=in_specs, out_specs=out_specs, check_vma=False)
```

```python
import jax
import jax.numpy as jnp
from jax import lax
from jax.experimental import pallas as pl
from jax.experimental.pallas import tpu as pltpu
from jax.sharding import PartitionSpec as P

LANES = 128
BRIEF = pl.CostEstimate(flops=1, bytes_accessed=1, transcendentals=0)
FIRST = (((0,), (0,)), ((), ()))
LAST = (((1,), (1,)), ((), ()))


def slot_table(routes_all, experts, n_expert, capacity):
    block, top = routes_all.shape
    flat_ids = routes_all.reshape(block * top)
    onehot = (flat_ids[:, None] == jnp.arange(experts, dtype=jnp.int32)[None, :]).astype(jnp.int32)
    before = jnp.sum(onehot * (jnp.cumsum(onehot, axis=0) - 1), axis=1)
    held = experts // n_expert
    owner = flat_ids // held
    local_index = flat_ids % held
    slot_of = ((local_index * n_expert + owner) * capacity + before).reshape(block, top)
    return jnp.arange(experts * capacity, dtype=jnp.int32)[:, None, None] == slot_of[None]


def expert_math(projected, back, gate_rows):
    gate_pre = projected[:, :, 0]
    up_value = projected[:, :, 1]
    sigmoid_gate = jax.nn.sigmoid(gate_pre)
    activated = gate_pre * sigmoid_gate
    hidden = activated * up_value
    gate_piece = jnp.sum(hidden * back, axis=2).astype(jnp.bfloat16)
    grad_hidden = gate_rows * back
    grad_pre = grad_hidden * up_value * sigmoid_gate * (1.0 + gate_pre * (1.0 - sigmoid_gate))
    grad_up = grad_hidden * activated
    grad_both = jnp.stack([grad_pre, grad_up], axis=2).astype(jnp.bfloat16)
    scaled_hidden = (gate_rows * hidden).astype(jnp.bfloat16)
    return (gate_piece, grad_both, scaled_hidden)


def routed_body(quant_tokens, token_scales, expert_ids, gate_weights, grad_out, w_in, w_out):
    tok_dev, width = quant_tokens.shape
    blocks = token_scales.shape[1]
    top = expert_ids.shape[1]
    n_tensor = lax.axis_size("tensor")
    n_expert = lax.axis_size("expert")
    held = w_in.shape[1]
    experts = held * n_expert
    block = tok_dev * n_tensor
    capacity = max(2, block * top * 13 // (12 * experts))
    rows = n_expert * capacity
    slots = experts * capacity
    share = width // n_tensor
    hidden_dev = w_out.shape[2]
    scaled = (
        (
            quant_tokens.astype(jnp.float32).reshape(tok_dev, blocks, width // blocks)
            * token_scales[:, :, None]
        )
        .reshape(tok_dev, width)
        .astype(jnp.bfloat16)
    )
    routes_all = lax.all_gather(expert_ids, "tensor", axis=0, tiled=True)
    routed = slot_table(routes_all, experts, n_expert, capacity)
    routed_float = routed.astype(jnp.float32)
    placing = jnp.any(routed, axis=2).astype(jnp.bfloat16)
    gates_all = lax.all_gather(gate_weights, "tensor", axis=0, tiled=True)
    tokens_part, cotangent_part = (
        lax.all_to_all(scaled, "tensor", split_axis=1, concat_axis=0, tiled=True),
        lax.all_to_all(grad_out, "tensor", split_axis=1, concat_axis=0, tiled=True),
    )
    slot_gates = jnp.einsum(
        "stk,tk->s", routed_float, gates_all.astype(jnp.float32), precision=lax.Precision.HIGHEST
    )
    slot_inputs = (
        jnp.dot(placing, tokens_part, preferred_element_type=jnp.float32)
        .astype(jnp.bfloat16)
        .reshape(held, n_expert, capacity, share)
    )
    slot_cotangent = (
        jnp.dot(placing, cotangent_part, preferred_element_type=jnp.float32)
        .astype(jnp.bfloat16)
        .reshape(held, n_expert, capacity, share)
    )
    part_inputs, part_cotangent, recv_gates = (
        lax.all_to_all(slot_inputs, "expert", split_axis=1, concat_axis=1, tiled=True),
        lax.all_to_all(slot_cotangent, "expert", split_axis=1, concat_axis=1, tiled=True),
        lax.all_to_all(
            slot_gates.astype(jnp.bfloat16).reshape(held, n_expert, capacity),
            "expert",
            split_axis=1,
            concat_axis=1,
            tiled=True,
        ),
    )
    recv_inputs, recv_cotangent = (
        lax.all_gather(part_inputs, "tensor", axis=3, tiled=True),
        lax.all_gather(part_cotangent, "tensor", axis=3, tiled=True),
    )
    inputs = recv_inputs.reshape(held, rows, width)
    cotangent = recv_cotangent.reshape(held, rows, width)
    gate_flat = recv_gates.reshape(held, rows).astype(jnp.float32)
    weights_in_all, weights_out_all = (
        lax.all_gather(w_in, "dp", axis=0, tiled=True),
        lax.all_gather(w_out, "dp", axis=0, tiled=True),
    )
    projected = jnp.einsum(
        "erd,dejh->erjh", inputs, weights_in_all, preferred_element_type=jnp.float32
    )
    back = jnp.einsum(
        "erd,deh->erh", cotangent, weights_out_all, preferred_element_type=jnp.float32
    )
    gate_piece, grad_both, scaled_hidden = expert_math(projected, back, gate_flat[:, :, None])
    token_piece = jnp.einsum(
        "erjh,dejh->erd", grad_both, weights_in_all, preferred_element_type=jnp.float32
    ).astype(jnp.bfloat16)
    term_in = jnp.einsum(
        "erd,erjh->dejh", inputs, grad_both, preferred_element_type=jnp.float32
    ).reshape(w_in.shape[0] * lax.axis_size("dp"), held, 2 * hidden_dev)
    term_out = jnp.einsum(
        "erd,erh->deh", cotangent, scaled_hidden, preferred_element_type=jnp.float32
    )
    summed = lax.psum_scatter(
        jnp.concatenate([term_in, term_out], axis=2).astype(jnp.bfloat16),
        "dp",
        scatter_dimension=0,
        tiled=True,
    ).astype(jnp.float32)
    grad_w_in = (
        summed[:, :, : 2 * hidden_dev]
        .astype(jnp.bfloat16)
        .reshape(w_in.shape[0], held, 2, hidden_dev)
    )
    grad_w_out = summed[:, :, 2 * hidden_dev :].astype(jnp.bfloat16)
    piece_float = (
        lax.optimization_barrier(token_piece)
        .astype(jnp.float32)
        .reshape(held, n_expert, capacity, width)
    )
    gate_float = (
        lax.optimization_barrier(gate_piece).astype(jnp.float32).reshape(held, n_expert, capacity)
    )
    slot_total = lax.psum_scatter(
        piece_float.astype(jnp.bfloat16), "tensor", scatter_dimension=3, tiled=True
    ).astype(jnp.float32)
    gate_total = lax.psum(gate_float, "tensor")
    back_cols, back_gates = (
        lax.all_to_all(
            slot_total.astype(jnp.bfloat16), "expert", split_axis=1, concat_axis=1, tiled=True
        ).astype(slot_total.dtype),
        lax.all_to_all(
            gate_total.astype(jnp.bfloat16), "expert", split_axis=1, concat_axis=1, tiled=True
        ).astype(gate_total.dtype),
    )
    token_cols_all = jnp.einsum(
        "st,sd->td",
        placing.astype(jnp.float32),
        back_cols.reshape(slots, share),
        precision=lax.Precision.HIGHEST,
    ).astype(jnp.bfloat16)
    grad_tokens = lax.all_to_all(token_cols_all, "tensor", split_axis=0, concat_axis=1, tiled=True)
    token_gate = jnp.einsum(
        "stk,s->tk", routed_float, back_gates.reshape(slots), precision=lax.Precision.HIGHEST
    )
    mine_gate = lax.dynamic_slice_in_dim(token_gate, lax.axis_index("tensor") * tok_dev, tok_dev, 0)
    return (grad_tokens, mine_gate, grad_w_in, grad_w_out)


def after(value, *others):
    return lax.optimization_barrier((value,) + others)[0]


def swap(array, stage):
    n_expert, n_tensor = lax.axis_size("expert"), lax.axis_size("tensor")
    pairs = []
    for e in range(n_expert):
        for t in range(n_tensor):
            axis, bit = stage[e & 1]
            e_to, t_to = (e ^ bit, t) if axis == "expert" else (e, t ^ bit)
            pairs.append((e * n_tensor + t, e_to * n_tensor + t_to))
    return lax.ppermute(array, ("expert", "tensor"), pairs)


def order_matrix(order, base, tok_dev):
    count = tok_dev << len(order)
    position = lax.broadcasted_iota(jnp.int32, (count, count), 1)
    block, offset = position // tok_dev, position % tok_dev
    top = len(order) - 1
    half = block >> top
    targets = []
    for core in range(2):
        where = [stage[core] for stage in base]
        target = half << top
        for place in range(top):
            bit = (block >> place) & 1
            target = target + (bit << where.index(order[place][core]))
        targets.append(target)
    owner = half ^ (lax.axis_index("expert") & 1)
    target = jnp.where(owner == 0, targets[0], targets[1])
    source = lax.broadcasted_iota(jnp.int32, (count, count), 0)
    return (source == target * tok_dev + offset).astype(jnp.bfloat16)


def pick_kernel(place, *refs):
    blocks, out = refs[:4], refs[-1]
    rows = jnp.concatenate([block[...] for block in blocks], axis=0)
    out[...] = jnp.dot(place[...], rows, preferred_element_type=jnp.float32).astype(jnp.bfloat16)


def pick(place, blocks, columns, start, width, so_far):
    slots, tokens = place.shape
    tile = 512
    first = start // tile
    kept = [pl.BlockSpec(memory_space=pl.ANY)] * len(so_far)
    return pl.pallas_call(
        pick_kernel,
        grid=(columns // tile,),
        in_specs=[pl.BlockSpec((slots, tokens), lambda i: (0, 0))]
        + [pl.BlockSpec((tokens // 4, tile), lambda i: (0, i))] * 4
        + kept,
        out_specs=pl.BlockSpec((slots, tile), lambda i: (0, first + i)),
        out_shape=jax.ShapeDtypeStruct((slots, width), jnp.bfloat16),
        input_output_aliases={5: 0} if so_far else {},
        compiler_params=pltpu.CompilerParams(vmem_limit_bytes=16 << 20),
        cost_estimate=pl.CostEstimate(
            flops=2 * slots * columns * tokens,
            bytes_accessed=2 * columns * (tokens + slots),
            transcendentals=0,
        ),
    )(place, *blocks, *so_far)


def weight_grad_kernel(inputs, cotangent, gate_grad, up_grad, scaled, *rest):
    grad_in, grad_out = rest[-2:]
    x, g = inputs[...], cotangent[...]
    grad_in[:, 0, :] = lax.dot_general(
        x, gate_grad[...], FIRST, preferred_element_type=jnp.float32
    ).astype(jnp.bfloat16)
    grad_in[:, 1, :] = lax.dot_general(
        x, up_grad[...], FIRST, preferred_element_type=jnp.float32
    ).astype(jnp.bfloat16)
    grad_out[...] = lax.dot_general(
        g, scaled[...], FIRST, preferred_element_type=jnp.float32
    ).astype(jnp.bfloat16)


def weight_grads(inputs, cotangent, gate_grad, up_grad, scaled, start, columns, so_far):
    rows, hidden = gate_grad.shape
    width = inputs.shape[1]
    tile = 512
    first = start // tile
    resident = pl.BlockSpec((rows, hidden), lambda i: (0, 0))
    stream = pl.BlockSpec((rows, tile), lambda i: (0, first + i))
    kept = [pl.BlockSpec(memory_space=pl.ANY)] * len(so_far)
    return pl.pallas_call(
        weight_grad_kernel,
        grid=(columns // tile,),
        in_specs=[stream, stream, resident, resident, resident] + kept,
        out_specs=[
            pl.BlockSpec((tile, 2, hidden), lambda i: (first + i, 0, 0)),
            pl.BlockSpec((tile, hidden), lambda i: (first + i, 0)),
        ],
        out_shape=[
            jax.ShapeDtypeStruct((width, 2, hidden), jnp.bfloat16),
            jax.ShapeDtypeStruct((width, hidden), jnp.bfloat16),
        ],
        input_output_aliases={5: 0, 6: 1} if so_far else {},
        compiler_params=pltpu.CompilerParams(vmem_limit_bytes=20 << 20),
        cost_estimate=BRIEF,
    )(inputs, cotangent, gate_grad, up_grad, scaled, *so_far)


def gathered_body(quant_tokens, token_scales, expert_ids, gate_weights, grad_out, w_in, w_out):
    tok_dev, width = quant_tokens.shape
    blocks = token_scales.shape[1]
    top = expert_ids.shape[1]
    n_tensor = lax.axis_size("tensor")
    n_expert = lax.axis_size("expert")
    tokens = tok_dev * n_tensor * n_expert
    half = tokens // 2
    capacity = max(2, tok_dev * n_tensor * top * 13 // (12 * n_expert))
    slots = n_expert * capacity
    hidden = w_out.shape[2]
    expert = lax.axis_index("expert")

    both = lambda *stages: [(s, s) for s in stages]
    core, across = ("expert", 1), ("expert", 2)
    along = both(*[("expert", 1 << k) for k in range(2, n_expert.bit_length() - 1)][::-1])
    sides = [("tensor", 1 << k) for k in range(n_tensor.bit_length() - 1)]
    one, two = sides + [across], [across] + sides
    crossed = list(zip(one, two))
    turned = list(zip(two, one))
    last = both(core)
    late = along + crossed + last
    early = turned + along + last
    mid = along[:1] + turned + along[1:] + last
    orders = dict(p=late, d=early, q=late, r=mid, s=late)
    unit = width // 10
    sizes = dict(p=6 * unit, d=4 * unit, q=10 * unit)
    starts = dict(p=0, d=6 * unit, q=0)
    spans = dict(r=(0, 5 * unit), s=(5 * unit, 10 * unit))
    base = orders["p"]

    scaled = (
        (
            quant_tokens.astype(jnp.float32).reshape(tok_dev, blocks, width // blocks)
            * token_scales[:, :, None]
        )
        .reshape(tok_dev, width)
        .astype(jnp.bfloat16)
    )
    routes = jnp.concatenate([expert_ids.astype(jnp.bfloat16), gate_weights], axis=1)
    routes = jnp.pad(routes, ((0, 0), (0, LANES - 2 * top)))

    rows = {}
    for name in "pdq":
        lo, hi = starts[name], starts[name] + sizes[name]
        part = scaled[:, lo:hi] if name in "pd" else grad_out[:, lo:hi]
        rows[name] = jnp.concatenate([part, routes], axis=1) if name == "d" else part

    tips = {}

    def step(name, *others):
        level = (rows[name].shape[0] // tok_dev).bit_length() - 1
        sent = after(rows[name], *others) if others else rows[name]
        got = swap(sent, orders[name][level])
        tips[name] = sent
        rows[name] = jnp.concatenate([sent, got], axis=0) if level < 3 else (sent, got)
        return got

    def finish(name, *others):
        low, high = rows[name]
        far_low = swap(after(low, *others[:-1]) if others[:-1] else low, last[0])
        far_high = swap(after(high, *others[-1:]) if others else high, last[0])
        rows[name] = (low, high, far_low, far_high)
        return far_high

    def make_routes():
        routes_all = jnp.concatenate([block[:, sizes["d"] :] for block in rows["d"]], axis=0)
        routes_all = jnp.dot(
            order_matrix(orders["d"], base, tok_dev),
            routes_all,
            preferred_element_type=jnp.float32,
        )
        lane = lax.broadcasted_iota(jnp.int32, routes_all.shape, 1)
        named = (routes_all == expert.astype(jnp.float32)) & (lane < top)
        chosen = jnp.any(named, axis=1, keepdims=True)
        gate_lanes = jnp.pad(routes_all[:, top:], ((0, 0), (0, top)))
        token_gate = jnp.sum(jnp.where(named, gate_lanes, 0.0), axis=1, keepdims=True)
        earlier = lax.broadcasted_iota(jnp.int32, (tokens, tokens), 0)
        later = lax.broadcasted_iota(jnp.int32, (tokens, tokens), 1)
        far = 2 * tokens
        ranking = jnp.where(earlier == later, -far, (earlier < later).astype(jnp.int32))
        ranking = ranking.astype(jnp.bfloat16)
        member = chosen.astype(jnp.bfloat16)
        rank = far + lax.dot_general(member, ranking, FIRST, preferred_element_type=jnp.float32)
        slot = lax.broadcasted_iota(jnp.int32, (slots, tokens), 0).astype(jnp.float32)
        placing = (slot == rank).astype(jnp.bfloat16)
        slot_gates = jnp.dot(
            placing, token_gate.astype(jnp.bfloat16), preferred_element_type=jnp.float32
        )
        placings = {}
        for name in orders:
            if orders[name] == base:
                placings[name] = placing
                continue
            moved = order_matrix(orders[name], base, tok_dev)
            placings[name] = jnp.dot(
                placing, moved, preferred_element_type=jnp.float32
            ).astype(jnp.bfloat16)
        return named, slot_gates, placings

    picked = dict(x=(), g=())

    def pick_step(name, *others):
        kind = "x" if name in "pd" else "g"
        place = after(placings[name], *others) if others else placings[name]
        picked[kind] = (
            pick(place, rows[name], sizes[name], starts[name], width, picked[kind]),
        )
        return picked[kind][0]

    def cut(name, *others):
        lo, hi = spans[name]
        return lax.optimization_barrier(after(w_in, *others)[lo:hi, 0])

    halves = {}
    p0 = step("p")
    q0 = step("q", tips["p"])
    d0 = step("d", tips["q"])
    p1 = step("p")
    d1 = step("d", p0)
    d2 = step("d")
    q1 = step("q", p1)
    p2 = step("p")
    halves["r"] = cut("r", tips["p"], tips["q"])
    p3 = step("p", halves["r"])
    d3 = step("d", p2)
    q2 = step("q", d2)
    halves["s"] = cut("s", tips["q"], tips["d"])
    finish("p", halves["s"])
    q3 = step("q", d3, halves["s"])
    finish("d")
    named, slot_gates, placings = make_routes()
    pick_step("p", tips["q"])
    inputs = pick_step("d", tips["q"])
    projected = 0.0
    for name in "rs":
        lo, hi = spans[name]
        projected += jnp.einsum(
            "rd,djh->rjh", inputs[:, lo:hi], halves[name], preferred_element_type=jnp.float32
        )
    gate_pre, up_value = projected[:, 0], projected[:, 1]
    finish("q", tips["q"], projected)
    cotangent = pick_step("q")
    back = jnp.dot(cotangent, w_out[:, 0], preferred_element_type=jnp.float32)

    sigmoid_gate = jax.nn.sigmoid(gate_pre)
    activated = gate_pre * sigmoid_gate
    hidden_value = activated * up_value
    gate_piece = jnp.sum(hidden_value * back, axis=1, keepdims=True).astype(jnp.bfloat16)
    grad_hidden = slot_gates * back
    gate_grad = (
        grad_hidden * up_value * sigmoid_gate * (1.0 + gate_pre * (1.0 - sigmoid_gate))
    ).astype(jnp.bfloat16)
    up_grad = (grad_hidden * activated).astype(jnp.bfloat16)
    scaled_hidden = (slot_gates * hidden_value).astype(jnp.bfloat16)

    grads = ()
    sums = {}

    def grad_step(low, high, *others):
        nonlocal grads
        left = after(gate_grad, *others) if others else gate_grad
        grads = weight_grads(
            inputs, cotangent, left, up_grad, scaled_hidden, low, high - low, grads
        )
        return grads[1]

    grad_both = jnp.stack([gate_grad, up_grad], axis=1)

    def piece_step(name, *others):
        lo, hi = spans[name]
        place = placings[name]
        left = after(grad_both, *others) if others else grad_both
        part = jnp.einsum(
            "rjh,djh->rd", left, halves[name], preferred_element_type=jnp.float32
        ).astype(jnp.bfloat16)
        put = lambda rows, kind: lax.dot_general(
            rows, part, FIRST, preferred_element_type=jnp.float32
        ).astype(kind)
        keep, send = put(place[:, :half], jnp.float32), put(place[:, half:], jnp.bfloat16)
        if name == "s":
            token_piece = lax.dot_general(
                place, gate_piece, FIRST, preferred_element_type=jnp.float32
            )
            extra = jnp.where(named, token_piece, 0.0)
            send = jnp.concatenate([send, extra[half:].astype(jnp.bfloat16)], axis=1)
            sums[name] = ([keep, extra[:half]], send)
        else:
            sums[name] = ([keep], send)
        return send

    def sum_step(name, *others):
        keeps, send = sums[name]
        level = (send.shape[0] // tok_dev).bit_length() - 1
        got = swap(send, orders[name][level])
        got = after(got, *others) if others else got
        count = send.shape[0] // 2
        at, new, out = 0, [], []
        for keep in keeps:
            total = keep + got[:, at : at + keep.shape[1]].astype(jnp.float32)
            at += keep.shape[1]
            new.append(total[:count] if level else total)
            out.append(total[count:].astype(jnp.bfloat16))
        send = (out[0] if len(out) == 1 else jnp.concatenate(out, axis=1)) if level else got
        sums[name] = (new, send)
        return send

    sr = piece_step("r")
    ss = piece_step("s", sr)
    r3 = sum_step("r")
    s3 = sum_step("s")
    g1 = grad_step(0, 4 * unit, s3)
    s2 = sum_step("s", g1)
    r2 = sum_step("r")
    g2 = grad_step(4 * unit, 6 * unit, r2)
    s1 = sum_step("s")
    r1 = sum_step("r", g2)
    g3 = grad_step(6 * unit, 8 * unit, r1)
    s0 = sum_step("s")
    r0 = sum_step("r", g3)
    g4 = grad_step(8 * unit, 10 * unit, r0)
    sum_step("s")
    sum_step("r", g4)

    grad_gates = sums["s"][0][1][:, :top]
    grad_tokens = jnp.concatenate([sums[n][0][0].astype(jnp.bfloat16) for n in "rs"], axis=1)
    return (
        grad_tokens,
        grad_gates,
        grads[0].reshape(width, 1, 2, hidden),
        grads[1].reshape(width, 1, hidden),
    )


def body(*arrays):
    quant_tokens, w_in = arrays[0], arrays[5]
    n_expert, n_tensor = lax.axis_size("expert"), lax.axis_size("tensor")
    whole = lax.axis_size("dp") == 1 and w_in.shape[1] == 1
    doubling = n_tensor == 2 and n_expert >= 8 and n_expert & (n_expert - 1) == 0
    few = quant_tokens.shape[0] * n_expert * n_tensor <= 1024
    tiled = quant_tokens.shape[1] % (10 * 512) == 0
    chosen = gathered_body if whole and doubling and few and tiled else routed_body
    return chosen(*arrays)


def solution(mesh):
    in_specs = (
        P(("dp", "expert", "tensor"), None),
        P(("dp", "expert", "tensor"), None),
        P(("dp", "expert", "tensor"), None),
        P(("dp", "expert", "tensor"), None),
        P(("dp", "expert", "tensor"), None),
        P("dp", "expert", None, "tensor"),
        P("dp", "expert", "tensor"),
    )
    out_specs = (
        P(("dp", "expert", "tensor"), None),
        P(("dp", "expert", "tensor"), None),
        P("dp", "expert", None, "tensor"),
        P("dp", "expert", "tensor"),
    )
    return jax.shard_map(body, mesh=mesh, in_specs=in_specs, out_specs=out_specs, check_vma=False)
```

```python
import jax
import jax.numpy as jnp
from jax import lax
from jax.experimental import pallas as pl
from jax.experimental.pallas import tpu as pltpu
from jax.sharding import PartitionSpec as P

LANES = 128
BRIEF = pl.CostEstimate(flops=1, bytes_accessed=1, transcendentals=0)
FIRST = (((0,), (0,)), ((), ()))
LAST = (((1,), (1,)), ((), ()))


def slot_table(routes_all, experts, n_expert, capacity):
    block, top = routes_all.shape
    flat_ids = routes_all.reshape(block * top)
    onehot = (flat_ids[:, None] == jnp.arange(experts, dtype=jnp.int32)[None, :]).astype(jnp.int32)
    before = jnp.sum(onehot * (jnp.cumsum(onehot, axis=0) - 1), axis=1)
    held = experts // n_expert
    owner = flat_ids // held
    local_index = flat_ids % held
    slot_of = ((local_index * n_expert + owner) * capacity + before).reshape(block, top)
    return jnp.arange(experts * capacity, dtype=jnp.int32)[:, None, None] == slot_of[None]


def expert_math(projected, back, gate_rows):
    gate_pre = projected[:, :, 0]
    up_value = projected[:, :, 1]
    sigmoid_gate = jax.nn.sigmoid(gate_pre)
    activated = gate_pre * sigmoid_gate
    hidden = activated * up_value
    gate_piece = jnp.sum(hidden * back, axis=2).astype(jnp.bfloat16)
    grad_hidden = gate_rows * back
    grad_pre = grad_hidden * up_value * sigmoid_gate * (1.0 + gate_pre * (1.0 - sigmoid_gate))
    grad_up = grad_hidden * activated
    grad_both = jnp.stack([grad_pre, grad_up], axis=2).astype(jnp.bfloat16)
    scaled_hidden = (gate_rows * hidden).astype(jnp.bfloat16)
    return (gate_piece, grad_both, scaled_hidden)


def routed_body(quant_tokens, token_scales, expert_ids, gate_weights, grad_out, w_in, w_out):
    tok_dev, width = quant_tokens.shape
    blocks = token_scales.shape[1]
    top = expert_ids.shape[1]
    n_tensor = lax.axis_size("tensor")
    n_expert = lax.axis_size("expert")
    held = w_in.shape[1]
    experts = held * n_expert
    block = tok_dev * n_tensor
    capacity = max(2, block * top * 13 // (12 * experts))
    rows = n_expert * capacity
    slots = experts * capacity
    share = width // n_tensor
    hidden_dev = w_out.shape[2]
    scaled = (
        (
            quant_tokens.astype(jnp.float32).reshape(tok_dev, blocks, width // blocks)
            * token_scales[:, :, None]
        )
        .reshape(tok_dev, width)
        .astype(jnp.bfloat16)
    )
    routes_all = lax.all_gather(expert_ids, "tensor", axis=0, tiled=True)
    routed = slot_table(routes_all, experts, n_expert, capacity)
    routed_float = routed.astype(jnp.float32)
    placing = jnp.any(routed, axis=2).astype(jnp.bfloat16)
    gates_all = lax.all_gather(gate_weights, "tensor", axis=0, tiled=True)
    tokens_part, cotangent_part = (
        lax.all_to_all(scaled, "tensor", split_axis=1, concat_axis=0, tiled=True),
        lax.all_to_all(grad_out, "tensor", split_axis=1, concat_axis=0, tiled=True),
    )
    slot_gates = jnp.einsum(
        "stk,tk->s", routed_float, gates_all.astype(jnp.float32), precision=lax.Precision.HIGHEST
    )
    slot_inputs = (
        jnp.dot(placing, tokens_part, preferred_element_type=jnp.float32)
        .astype(jnp.bfloat16)
        .reshape(held, n_expert, capacity, share)
    )
    slot_cotangent = (
        jnp.dot(placing, cotangent_part, preferred_element_type=jnp.float32)
        .astype(jnp.bfloat16)
        .reshape(held, n_expert, capacity, share)
    )
    part_inputs, part_cotangent, recv_gates = (
        lax.all_to_all(slot_inputs, "expert", split_axis=1, concat_axis=1, tiled=True),
        lax.all_to_all(slot_cotangent, "expert", split_axis=1, concat_axis=1, tiled=True),
        lax.all_to_all(
            slot_gates.astype(jnp.bfloat16).reshape(held, n_expert, capacity),
            "expert",
            split_axis=1,
            concat_axis=1,
            tiled=True,
        ),
    )
    recv_inputs, recv_cotangent = (
        lax.all_gather(part_inputs, "tensor", axis=3, tiled=True),
        lax.all_gather(part_cotangent, "tensor", axis=3, tiled=True),
    )
    inputs = recv_inputs.reshape(held, rows, width)
    cotangent = recv_cotangent.reshape(held, rows, width)
    gate_flat = recv_gates.reshape(held, rows).astype(jnp.float32)
    weights_in_all, weights_out_all = (
        lax.all_gather(w_in, "dp", axis=0, tiled=True),
        lax.all_gather(w_out, "dp", axis=0, tiled=True),
    )
    projected = jnp.einsum(
        "erd,dejh->erjh", inputs, weights_in_all, preferred_element_type=jnp.float32
    )
    back = jnp.einsum(
        "erd,deh->erh", cotangent, weights_out_all, preferred_element_type=jnp.float32
    )
    gate_piece, grad_both, scaled_hidden = expert_math(projected, back, gate_flat[:, :, None])
    token_piece = jnp.einsum(
        "erjh,dejh->erd", grad_both, weights_in_all, preferred_element_type=jnp.float32
    ).astype(jnp.bfloat16)
    term_in = jnp.einsum(
        "erd,erjh->dejh", inputs, grad_both, preferred_element_type=jnp.float32
    ).reshape(w_in.shape[0] * lax.axis_size("dp"), held, 2 * hidden_dev)
    term_out = jnp.einsum(
        "erd,erh->deh", cotangent, scaled_hidden, preferred_element_type=jnp.float32
    )
    summed = lax.psum_scatter(
        jnp.concatenate([term_in, term_out], axis=2).astype(jnp.bfloat16),
        "dp",
        scatter_dimension=0,
        tiled=True,
    ).astype(jnp.float32)
    grad_w_in = (
        summed[:, :, : 2 * hidden_dev]
        .astype(jnp.bfloat16)
        .reshape(w_in.shape[0], held, 2, hidden_dev)
    )
    grad_w_out = summed[:, :, 2 * hidden_dev :].astype(jnp.bfloat16)
    piece_float = (
        lax.optimization_barrier(token_piece)
        .astype(jnp.float32)
        .reshape(held, n_expert, capacity, width)
    )
    gate_float = (
        lax.optimization_barrier(gate_piece).astype(jnp.float32).reshape(held, n_expert, capacity)
    )
    slot_total = lax.psum_scatter(
        piece_float.astype(jnp.bfloat16), "tensor", scatter_dimension=3, tiled=True
    ).astype(jnp.float32)
    gate_total = lax.psum(gate_float, "tensor")
    back_cols, back_gates = (
        lax.all_to_all(
            slot_total.astype(jnp.bfloat16), "expert", split_axis=1, concat_axis=1, tiled=True
        ).astype(slot_total.dtype),
        lax.all_to_all(
            gate_total.astype(jnp.bfloat16), "expert", split_axis=1, concat_axis=1, tiled=True
        ).astype(gate_total.dtype),
    )
    token_cols_all = jnp.einsum(
        "st,sd->td",
        placing.astype(jnp.float32),
        back_cols.reshape(slots, share),
        precision=lax.Precision.HIGHEST,
    ).astype(jnp.bfloat16)
    grad_tokens = lax.all_to_all(token_cols_all, "tensor", split_axis=0, concat_axis=1, tiled=True)
    token_gate = jnp.einsum(
        "stk,s->tk", routed_float, back_gates.reshape(slots), precision=lax.Precision.HIGHEST
    )
    mine_gate = lax.dynamic_slice_in_dim(token_gate, lax.axis_index("tensor") * tok_dev, tok_dev, 0)
    return (grad_tokens, mine_gate, grad_w_in, grad_w_out)


def after(value, *others):
    return lax.optimization_barrier((value,) + others)[0]


def swap(array, stage):
    n_expert, n_tensor = lax.axis_size("expert"), lax.axis_size("tensor")
    pairs = []
    for e in range(n_expert):
        for t in range(n_tensor):
            axis, bit = stage[e & 1]
            e_to, t_to = (e ^ bit, t) if axis == "expert" else (e, t ^ bit)
            pairs.append((e * n_tensor + t, e_to * n_tensor + t_to))
    return lax.ppermute(array, ("expert", "tensor"), pairs)


def order_matrix(order, base, tok_dev):
    count = tok_dev << len(order)
    position = lax.broadcasted_iota(jnp.int32, (count, count), 1)
    block, offset = position // tok_dev, position % tok_dev
    top = len(order) - 1
    half = block >> top
    targets = []
    for core in range(2):
        where = [stage[core] for stage in base]
        target = half << top
        for place in range(top):
            bit = (block >> place) & 1
            target = target + (bit << where.index(order[place][core]))
        targets.append(target)
    owner = half ^ (lax.axis_index("expert") & 1)
    target = jnp.where(owner == 0, targets[0], targets[1])
    source = lax.broadcasted_iota(jnp.int32, (count, count), 0)
    return (source == target * tok_dev + offset).astype(jnp.bfloat16)


def pick_kernel(place, *refs):
    blocks, out = refs[:4], refs[-1]
    rows = jnp.concatenate([block[...] for block in blocks], axis=0)
    out[...] = jnp.dot(place[...], rows, preferred_element_type=jnp.float32).astype(jnp.bfloat16)


def pick(place, blocks, columns, start, width, so_far):
    slots, tokens = place.shape
    tile = 1024
    first = start // tile
    kept = [pl.BlockSpec(memory_space=pl.ANY)] * len(so_far)
    return pl.pallas_call(
        pick_kernel,
        grid=(columns // tile,),
        in_specs=[pl.BlockSpec((slots, tokens), lambda i: (0, 0))]
        + [pl.BlockSpec((tokens // 4, tile), lambda i: (0, i))] * 4
        + kept,
        out_specs=pl.BlockSpec((slots, tile), lambda i: (0, first + i)),
        out_shape=jax.ShapeDtypeStruct((slots, width), jnp.bfloat16),
        input_output_aliases={5: 0} if so_far else {},
        compiler_params=pltpu.CompilerParams(vmem_limit_bytes=7 << 20),
        cost_estimate=BRIEF,
    )(place, *blocks, *so_far)


def weight_grad_kernel(inputs, cotangent, gate_grad, up_grad, scaled, *rest):
    grad_in, grad_out = rest[-2:]
    x, g = inputs[...], cotangent[...]
    grad_in[:, 0, :] = lax.dot_general(
        x, gate_grad[...], FIRST, preferred_element_type=jnp.float32
    ).astype(jnp.bfloat16)
    grad_in[:, 1, :] = lax.dot_general(
        x, up_grad[...], FIRST, preferred_element_type=jnp.float32
    ).astype(jnp.bfloat16)
    grad_out[...] = lax.dot_general(
        g, scaled[...], FIRST, preferred_element_type=jnp.float32
    ).astype(jnp.bfloat16)


def weight_grads(inputs, cotangent, gate_grad, up_grad, scaled, start, columns, so_far):
    rows, hidden = gate_grad.shape
    width = inputs.shape[1]
    tile = 512
    first = start // tile
    resident = pl.BlockSpec((rows, hidden), lambda i: (0, 0))
    stream = pl.BlockSpec((rows, tile), lambda i: (0, first + i))
    kept = [pl.BlockSpec(memory_space=pl.ANY)] * len(so_far)
    return pl.pallas_call(
        weight_grad_kernel,
        grid=(columns // tile,),
        in_specs=[stream, stream, resident, resident, resident] + kept,
        out_specs=[
            pl.BlockSpec((tile, 2, hidden), lambda i: (first + i, 0, 0)),
            pl.BlockSpec((tile, hidden), lambda i: (first + i, 0)),
        ],
        out_shape=[
            jax.ShapeDtypeStruct((width, 2, hidden), jnp.bfloat16),
            jax.ShapeDtypeStruct((width, hidden), jnp.bfloat16),
        ],
        input_output_aliases={5: 0, 6: 1} if so_far else {},
        compiler_params=pltpu.CompilerParams(vmem_limit_bytes=20 << 20),
        cost_estimate=BRIEF,
    )(inputs, cotangent, gate_grad, up_grad, scaled, *so_far)


def gathered_body(quant_tokens, token_scales, expert_ids, gate_weights, grad_out, w_in, w_out):
    tok_dev, width = quant_tokens.shape
    blocks = token_scales.shape[1]
    top = expert_ids.shape[1]
    n_tensor = lax.axis_size("tensor")
    n_expert = lax.axis_size("expert")
    tokens = tok_dev * n_tensor * n_expert
    half = tokens // 2
    capacity = max(2, tok_dev * n_tensor * top * 13 // (12 * n_expert))
    slots = n_expert * capacity
    hidden = w_out.shape[2]
    expert = lax.axis_index("expert")

    both = lambda *stages: [(s, s) for s in stages]
    core, across = ("expert", 1), ("expert", 2)
    along = both(*[("expert", 1 << k) for k in range(2, n_expert.bit_length() - 1)][::-1])
    sides = [("tensor", 1 << k) for k in range(n_tensor.bit_length() - 1)]
    one, two = sides + [across], [across] + sides
    crossed = list(zip(one, two))
    turned = list(zip(two, one))
    last = both(core)
    late = along + crossed + last
    early = turned + along + last
    mid = along[:1] + turned + along[1:] + last
    orders = dict(p=late, d=early, q=late, r=mid, s=late)
    unit = width // 10
    sizes = dict(p=6 * unit, d=4 * unit, q=10 * unit)
    starts = dict(p=0, d=6 * unit, q=0)
    spans = dict(r=(0, 5 * unit), s=(5 * unit, 10 * unit))
    base = orders["p"]

    scaled = (
        (
            quant_tokens.astype(jnp.float32).reshape(tok_dev, blocks, width // blocks)
            * token_scales[:, :, None]
        )
        .reshape(tok_dev, width)
        .astype(jnp.bfloat16)
    )
    routes = jnp.concatenate([expert_ids.astype(jnp.bfloat16), gate_weights], axis=1)
    routes = jnp.pad(routes, ((0, 0), (0, LANES - 2 * top)))

    rows = {}
    for name in "pdq":
        lo, hi = starts[name], starts[name] + sizes[name]
        part = scaled[:, lo:hi] if name in "pd" else grad_out[:, lo:hi]
        rows[name] = jnp.concatenate([part, routes], axis=1) if name == "d" else part

    tips = {}

    def step(name, *others):
        level = (rows[name].shape[0] // tok_dev).bit_length() - 1
        sent = after(rows[name], *others) if others else rows[name]
        got = swap(sent, orders[name][level])
        tips[name] = sent
        rows[name] = jnp.concatenate([sent, got], axis=0) if level < 3 else (sent, got)
        return got

    def finish(name, *others):
        low, high = rows[name]
        far_low = swap(after(low, *others[:-1]) if others[:-1] else low, last[0])
        far_high = swap(after(high, *others[-1:]) if others else high, last[0])
        rows[name] = (low, high, far_low, far_high)
        return far_high

    def make_routes():
        routes_all = jnp.concatenate([block[:, sizes["d"] :] for block in rows["d"]], axis=0)
        routes_all = jnp.dot(
            order_matrix(orders["d"], base, tok_dev),
            routes_all,
            preferred_element_type=jnp.float32,
        )
        lane = lax.broadcasted_iota(jnp.int32, routes_all.shape, 1)
        named = (routes_all == expert.astype(jnp.float32)) & (lane < top)
        chosen = jnp.any(named, axis=1, keepdims=True)
        gate_lanes = jnp.pad(routes_all[:, top:], ((0, 0), (0, top)))
        token_gate = jnp.sum(jnp.where(named, gate_lanes, 0.0), axis=1, keepdims=True)
        earlier = lax.broadcasted_iota(jnp.int32, (tokens, tokens), 0)
        later = lax.broadcasted_iota(jnp.int32, (tokens, tokens), 1)
        far = 2 * tokens
        ranking = jnp.where(earlier == later, -far, (earlier < later).astype(jnp.int32))
        ranking = ranking.astype(jnp.bfloat16)
        member = chosen.astype(jnp.bfloat16)
        rank = far + lax.dot_general(member, ranking, FIRST, preferred_element_type=jnp.float32)
        slot = lax.broadcasted_iota(jnp.int32, (slots, tokens), 0).astype(jnp.float32)
        placing = (slot == rank).astype(jnp.bfloat16)
        slot_gates = jnp.dot(
            placing, token_gate.astype(jnp.bfloat16), preferred_element_type=jnp.float32
        )
        placings = {}
        for name in orders:
            if orders[name] == base:
                placings[name] = placing
                continue
            moved = order_matrix(orders[name], base, tok_dev)
            placings[name] = jnp.dot(
                placing, moved, preferred_element_type=jnp.float32
            ).astype(jnp.bfloat16)
        return named, slot_gates, placings

    picked = dict(x=(), g=())

    def pick_step(name, *others):
        kind = "x" if name in "pd" else "g"
        place = after(placings[name], *others) if others else placings[name]
        picked[kind] = (
            pick(place, rows[name], sizes[name], starts[name], width, picked[kind]),
        )
        return picked[kind][0]

    def cut(name, *others):
        lo, hi = spans[name]
        return lax.optimization_barrier(after(w_in, *others)[lo:hi, 0])

    halves = {}
    p0 = step("p")
    q0 = step("q", tips["p"])
    d0 = step("d", tips["q"])
    p1 = step("p")
    d1 = step("d", p0)
    d2 = step("d")
    q1 = step("q", p1)
    p2 = step("p")
    halves["r"] = cut("r", tips["p"], tips["q"])
    p3 = step("p", halves["r"])
    d3 = step("d", p2)
    q2 = step("q", d2)
    halves["s"] = cut("s", tips["q"], tips["d"])
    finish("p", halves["s"])
    q3 = step("q", d3, halves["s"])
    finish("d")
    named, slot_gates, placings = make_routes()
    pick_step("p", tips["q"])
    inputs = pick_step("d", tips["q"])
    projected = 0.0
    for name in "rs":
        lo, hi = spans[name]
        projected += jnp.einsum(
            "rd,djh->rjh", inputs[:, lo:hi], halves[name], preferred_element_type=jnp.float32
        )
    gate_pre, up_value = projected[:, 0], projected[:, 1]
    finish("q", tips["q"], projected)
    cotangent = pick_step("q")
    back = jnp.dot(cotangent, w_out[:, 0], preferred_element_type=jnp.float32)

    sigmoid_gate = jax.nn.sigmoid(gate_pre)
    activated = gate_pre * sigmoid_gate
    hidden_value = activated * up_value
    gate_piece = jnp.sum(hidden_value * back, axis=1, keepdims=True).astype(jnp.bfloat16)
    grad_hidden = slot_gates * back
    gate_grad = (
        grad_hidden * up_value * sigmoid_gate * (1.0 + gate_pre * (1.0 - sigmoid_gate))
    ).astype(jnp.bfloat16)
    up_grad = (grad_hidden * activated).astype(jnp.bfloat16)
    scaled_hidden = (slot_gates * hidden_value).astype(jnp.bfloat16)

    grads = ()
    sums = {}

    def grad_step(low, high, *others):
        nonlocal grads
        left = after(gate_grad, *others) if others else gate_grad
        grads = weight_grads(
            inputs, cotangent, left, up_grad, scaled_hidden, low, high - low, grads
        )
        return grads[1]

    grad_both = jnp.stack([gate_grad, up_grad], axis=1)

    def piece_step(name, *others):
        lo, hi = spans[name]
        place = placings[name]
        left = after(grad_both, *others) if others else grad_both
        part = jnp.einsum(
            "rjh,djh->rd", left, halves[name], preferred_element_type=jnp.float32
        ).astype(jnp.bfloat16)
        put = lambda rows, kind: lax.dot_general(
            rows, part, FIRST, preferred_element_type=jnp.float32
        ).astype(kind)
        keep, send = put(place[:, :half], jnp.float32), put(place[:, half:], jnp.bfloat16)
        if name == "s":
            token_piece = lax.dot_general(
                place, gate_piece, FIRST, preferred_element_type=jnp.float32
            )
            extra = jnp.where(named, token_piece, 0.0)
            send = jnp.concatenate([send, extra[half:].astype(jnp.bfloat16)], axis=1)
            sums[name] = ([keep, extra[:half]], send)
        else:
            sums[name] = ([keep], send)
        return send

    def sum_step(name, *others):
        keeps, send = sums[name]
        level = (send.shape[0] // tok_dev).bit_length() - 1
        got = swap(send, orders[name][level])
        got = after(got, *others) if others else got
        count = send.shape[0] // 2
        at, new, out = 0, [], []
        for keep in keeps:
            total = keep + got[:, at : at + keep.shape[1]].astype(jnp.float32)
            at += keep.shape[1]
            new.append(total[:count] if level else total)
            out.append(total[count:].astype(jnp.bfloat16))
        send = (out[0] if len(out) == 1 else jnp.concatenate(out, axis=1)) if level else got
        sums[name] = (new, send)
        return send

    sr = piece_step("r")
    ss = piece_step("s", sr)
    r3 = sum_step("r")
    s3 = sum_step("s")
    g1 = grad_step(0, 4 * unit, s3)
    s2 = sum_step("s", g1)
    r2 = sum_step("r")
    g2 = grad_step(4 * unit, 6 * unit, r2)
    s1 = sum_step("s")
    r1 = sum_step("r", g2)
    g3 = grad_step(6 * unit, 8 * unit, r1)
    s0 = sum_step("s")
    r0 = sum_step("r", g3)
    g4 = grad_step(8 * unit, 10 * unit, r0)
    sum_step("s")
    sum_step("r", g4)

    grad_gates = sums["s"][0][1][:, :top]
    grad_tokens = jnp.concatenate([sums[n][0][0].astype(jnp.bfloat16) for n in "rs"], axis=1)
    return (
        grad_tokens,
        grad_gates,
        grads[0].reshape(width, 1, 2, hidden),
        grads[1].reshape(width, 1, hidden),
    )


def body(*arrays):
    quant_tokens, w_in = arrays[0], arrays[5]
    n_expert, n_tensor = lax.axis_size("expert"), lax.axis_size("tensor")
    whole = lax.axis_size("dp") == 1 and w_in.shape[1] == 1
    doubling = n_tensor == 2 and n_expert >= 8 and n_expert & (n_expert - 1) == 0
    few = quant_tokens.shape[0] * n_expert * n_tensor <= 1024
    tiled = quant_tokens.shape[1] % (10 * 512) == 0
    chosen = gathered_body if whole and doubling and few and tiled else routed_body
    return chosen(*arrays)


def solution(mesh):
    in_specs = (
        P(("dp", "expert", "tensor"), None),
        P(("dp", "expert", "tensor"), None),
        P(("dp", "expert", "tensor"), None),
        P(("dp", "expert", "tensor"), None),
        P(("dp", "expert", "tensor"), None),
        P("dp", "expert", None, "tensor"),
        P("dp", "expert", "tensor"),
    )
    out_specs = (
        P(("dp", "expert", "tensor"), None),
        P(("dp", "expert", "tensor"), None),
        P("dp", "expert", None, "tensor"),
        P("dp", "expert", "tensor"),
    )
    return jax.shard_map(body, mesh=mesh, in_specs=in_specs, out_specs=out_specs, check_vma=False)
```

```python
import jax
import jax.numpy as jnp
from jax import lax
from jax.experimental import pallas as pl
from jax.experimental.pallas import tpu as pltpu
from jax.sharding import PartitionSpec as P

LANES = 128
BRIEF = pl.CostEstimate(flops=1, bytes_accessed=1, transcendentals=0)
FIRST = (((0,), (0,)), ((), ()))
LAST = (((1,), (1,)), ((), ()))


def slot_table(routes_all, experts, n_expert, capacity):
    block, top = routes_all.shape
    flat_ids = routes_all.reshape(block * top)
    onehot = (flat_ids[:, None] == jnp.arange(experts, dtype=jnp.int32)[None, :]).astype(jnp.int32)
    before = jnp.sum(onehot * (jnp.cumsum(onehot, axis=0) - 1), axis=1)
    held = experts // n_expert
    owner = flat_ids // held
    local_index = flat_ids % held
    slot_of = ((local_index * n_expert + owner) * capacity + before).reshape(block, top)
    return jnp.arange(experts * capacity, dtype=jnp.int32)[:, None, None] == slot_of[None]


def expert_math(projected, back, gate_rows):
    gate_pre = projected[:, :, 0]
    up_value = projected[:, :, 1]
    sigmoid_gate = jax.nn.sigmoid(gate_pre)
    activated = gate_pre * sigmoid_gate
    hidden = activated * up_value
    gate_piece = jnp.sum(hidden * back, axis=2).astype(jnp.bfloat16)
    grad_hidden = gate_rows * back
    grad_pre = grad_hidden * up_value * sigmoid_gate * (1.0 + gate_pre * (1.0 - sigmoid_gate))
    grad_up = grad_hidden * activated
    grad_both = jnp.stack([grad_pre, grad_up], axis=2).astype(jnp.bfloat16)
    scaled_hidden = (gate_rows * hidden).astype(jnp.bfloat16)
    return (gate_piece, grad_both, scaled_hidden)


def routed_body(quant_tokens, token_scales, expert_ids, gate_weights, grad_out, w_in, w_out):
    tok_dev, width = quant_tokens.shape
    blocks = token_scales.shape[1]
    top = expert_ids.shape[1]
    n_tensor = lax.axis_size("tensor")
    n_expert = lax.axis_size("expert")
    held = w_in.shape[1]
    experts = held * n_expert
    block = tok_dev * n_tensor
    capacity = max(2, block * top * 13 // (12 * experts))
    rows = n_expert * capacity
    slots = experts * capacity
    share = width // n_tensor
    hidden_dev = w_out.shape[2]
    scaled = (
        (
            quant_tokens.astype(jnp.float32).reshape(tok_dev, blocks, width // blocks)
            * token_scales[:, :, None]
        )
        .reshape(tok_dev, width)
        .astype(jnp.bfloat16)
    )
    routes_all = lax.all_gather(expert_ids, "tensor", axis=0, tiled=True)
    routed = slot_table(routes_all, experts, n_expert, capacity)
    routed_float = routed.astype(jnp.float32)
    placing = jnp.any(routed, axis=2).astype(jnp.bfloat16)
    gates_all = lax.all_gather(gate_weights, "tensor", axis=0, tiled=True)
    tokens_part, cotangent_part = (
        lax.all_to_all(scaled, "tensor", split_axis=1, concat_axis=0, tiled=True),
        lax.all_to_all(grad_out, "tensor", split_axis=1, concat_axis=0, tiled=True),
    )
    slot_gates = jnp.einsum(
        "stk,tk->s", routed_float, gates_all.astype(jnp.float32), precision=lax.Precision.HIGHEST
    )
    slot_inputs = (
        jnp.dot(placing, tokens_part, preferred_element_type=jnp.float32)
        .astype(jnp.bfloat16)
        .reshape(held, n_expert, capacity, share)
    )
    slot_cotangent = (
        jnp.dot(placing, cotangent_part, preferred_element_type=jnp.float32)
        .astype(jnp.bfloat16)
        .reshape(held, n_expert, capacity, share)
    )
    part_inputs, part_cotangent, recv_gates = (
        lax.all_to_all(slot_inputs, "expert", split_axis=1, concat_axis=1, tiled=True),
        lax.all_to_all(slot_cotangent, "expert", split_axis=1, concat_axis=1, tiled=True),
        lax.all_to_all(
            slot_gates.astype(jnp.bfloat16).reshape(held, n_expert, capacity),
            "expert",
            split_axis=1,
            concat_axis=1,
            tiled=True,
        ),
    )
    recv_inputs, recv_cotangent = (
        lax.all_gather(part_inputs, "tensor", axis=3, tiled=True),
        lax.all_gather(part_cotangent, "tensor", axis=3, tiled=True),
    )
    inputs = recv_inputs.reshape(held, rows, width)
    cotangent = recv_cotangent.reshape(held, rows, width)
    gate_flat = recv_gates.reshape(held, rows).astype(jnp.float32)
    weights_in_all, weights_out_all = (
        lax.all_gather(w_in, "dp", axis=0, tiled=True),
        lax.all_gather(w_out, "dp", axis=0, tiled=True),
    )
    projected = jnp.einsum(
        "erd,dejh->erjh", inputs, weights_in_all, preferred_element_type=jnp.float32
    )
    back = jnp.einsum(
        "erd,deh->erh", cotangent, weights_out_all, preferred_element_type=jnp.float32
    )
    gate_piece, grad_both, scaled_hidden = expert_math(projected, back, gate_flat[:, :, None])
    token_piece = jnp.einsum(
        "erjh,dejh->erd", grad_both, weights_in_all, preferred_element_type=jnp.float32
    ).astype(jnp.bfloat16)
    term_in = jnp.einsum(
        "erd,erjh->dejh", inputs, grad_both, preferred_element_type=jnp.float32
    ).reshape(w_in.shape[0] * lax.axis_size("dp"), held, 2 * hidden_dev)
    term_out = jnp.einsum(
        "erd,erh->deh", cotangent, scaled_hidden, preferred_element_type=jnp.float32
    )
    summed = lax.psum_scatter(
        jnp.concatenate([term_in, term_out], axis=2).astype(jnp.bfloat16),
        "dp",
        scatter_dimension=0,
        tiled=True,
    ).astype(jnp.float32)
    grad_w_in = (
        summed[:, :, : 2 * hidden_dev]
        .astype(jnp.bfloat16)
        .reshape(w_in.shape[0], held, 2, hidden_dev)
    )
    grad_w_out = summed[:, :, 2 * hidden_dev :].astype(jnp.bfloat16)
    piece_float = (
        lax.optimization_barrier(token_piece)
        .astype(jnp.float32)
        .reshape(held, n_expert, capacity, width)
    )
    gate_float = (
        lax.optimization_barrier(gate_piece).astype(jnp.float32).reshape(held, n_expert, capacity)
    )
    slot_total = lax.psum_scatter(
        piece_float.astype(jnp.bfloat16), "tensor", scatter_dimension=3, tiled=True
    ).astype(jnp.float32)
    gate_total = lax.psum(gate_float, "tensor")
    back_cols, back_gates = (
        lax.all_to_all(
            slot_total.astype(jnp.bfloat16), "expert", split_axis=1, concat_axis=1, tiled=True
        ).astype(slot_total.dtype),
        lax.all_to_all(
            gate_total.astype(jnp.bfloat16), "expert", split_axis=1, concat_axis=1, tiled=True
        ).astype(gate_total.dtype),
    )
    token_cols_all = jnp.einsum(
        "st,sd->td",
        placing.astype(jnp.float32),
        back_cols.reshape(slots, share),
        precision=lax.Precision.HIGHEST,
    ).astype(jnp.bfloat16)
    grad_tokens = lax.all_to_all(token_cols_all, "tensor", split_axis=0, concat_axis=1, tiled=True)
    token_gate = jnp.einsum(
        "stk,s->tk", routed_float, back_gates.reshape(slots), precision=lax.Precision.HIGHEST
    )
    mine_gate = lax.dynamic_slice_in_dim(token_gate, lax.axis_index("tensor") * tok_dev, tok_dev, 0)
    return (grad_tokens, mine_gate, grad_w_in, grad_w_out)


def after(value, *others):
    return lax.optimization_barrier((value,) + others)[0]


def swap(array, stage):
    n_expert, n_tensor = lax.axis_size("expert"), lax.axis_size("tensor")
    pairs = []
    for e in range(n_expert):
        for t in range(n_tensor):
            axis, bit = stage[e & 1]
            e_to, t_to = (e ^ bit, t) if axis == "expert" else (e, t ^ bit)
            pairs.append((e * n_tensor + t, e_to * n_tensor + t_to))
    return lax.ppermute(array, ("expert", "tensor"), pairs)


def order_matrix(order, base, tok_dev):
    count = tok_dev << len(order)
    position = lax.broadcasted_iota(jnp.int32, (count, count), 1)
    block, offset = position // tok_dev, position % tok_dev
    top = len(order) - 1
    half = block >> top
    targets = []
    for core in range(2):
        where = [stage[core] for stage in base]
        target = half << top
        for place in range(top):
            bit = (block >> place) & 1
            target = target + (bit << where.index(order[place][core]))
        targets.append(target)
    owner = half ^ (lax.axis_index("expert") & 1)
    target = jnp.where(owner == 0, targets[0], targets[1])
    source = lax.broadcasted_iota(jnp.int32, (count, count), 0)
    return (source == target * tok_dev + offset).astype(jnp.bfloat16)


def pick_kernel(place, *refs):
    blocks, out = refs[:4], refs[-1]
    rows = jnp.concatenate([block[...] for block in blocks], axis=0)
    out[...] = jnp.dot(place[...], rows, preferred_element_type=jnp.float32).astype(jnp.bfloat16)


def pick(place, blocks, columns, start, width, so_far):
    slots, tokens = place.shape
    tile = 1024
    first = start // tile
    kept = [pl.BlockSpec(memory_space=pl.ANY)] * len(so_far)
    return pl.pallas_call(
        pick_kernel,
        grid=(columns // tile,),
        in_specs=[pl.BlockSpec((slots, tokens), lambda i: (0, 0))]
        + [pl.BlockSpec((tokens // 4, tile), lambda i: (0, i))] * 4
        + kept,
        out_specs=pl.BlockSpec((slots, tile), lambda i: (0, first + i)),
        out_shape=jax.ShapeDtypeStruct((slots, width), jnp.bfloat16),
        input_output_aliases={5: 0} if so_far else {},
        compiler_params=pltpu.CompilerParams(vmem_limit_bytes=7 << 20),
        cost_estimate=BRIEF,
    )(place, *blocks, *so_far)


def weight_grad_kernel(inputs, cotangent, gate_grad, up_grad, scaled, *rest):
    grad_in, grad_out = rest[-2:]
    x, g = inputs[...], cotangent[...]
    grad_in[:, 0, :] = lax.dot_general(
        x, gate_grad[...], FIRST, preferred_element_type=jnp.float32
    ).astype(jnp.bfloat16)
    grad_in[:, 1, :] = lax.dot_general(
        x, up_grad[...], FIRST, preferred_element_type=jnp.float32
    ).astype(jnp.bfloat16)
    grad_out[...] = lax.dot_general(
        g, scaled[...], FIRST, preferred_element_type=jnp.float32
    ).astype(jnp.bfloat16)


def weight_grads(inputs, cotangent, gate_grad, up_grad, scaled, start, columns, so_far):
    rows, hidden = gate_grad.shape
    width = inputs.shape[1]
    tile = 512
    first = start // tile
    resident = pl.BlockSpec((rows, hidden), lambda i: (0, 0))
    stream = pl.BlockSpec((rows, tile), lambda i: (0, first + i))
    kept = [pl.BlockSpec(memory_space=pl.ANY)] * len(so_far)
    return pl.pallas_call(
        weight_grad_kernel,
        grid=(columns // tile,),
        in_specs=[stream, stream, resident, resident, resident] + kept,
        out_specs=[
            pl.BlockSpec((tile, 2, hidden), lambda i: (first + i, 0, 0)),
            pl.BlockSpec((tile, hidden), lambda i: (first + i, 0)),
        ],
        out_shape=[
            jax.ShapeDtypeStruct((width, 2, hidden), jnp.bfloat16),
            jax.ShapeDtypeStruct((width, hidden), jnp.bfloat16),
        ],
        input_output_aliases={5: 0, 6: 1} if so_far else {},
        compiler_params=pltpu.CompilerParams(vmem_limit_bytes=20 << 20),
        cost_estimate=BRIEF,
    )(inputs, cotangent, gate_grad, up_grad, scaled, *so_far)


def gathered_body(quant_tokens, token_scales, expert_ids, gate_weights, grad_out, w_in, w_out):
    tok_dev, width = quant_tokens.shape
    blocks = token_scales.shape[1]
    top = expert_ids.shape[1]
    n_tensor = lax.axis_size("tensor")
    n_expert = lax.axis_size("expert")
    tokens = tok_dev * n_tensor * n_expert
    half = tokens // 2
    capacity = max(2, tok_dev * n_tensor * top * 13 // (12 * n_expert))
    slots = n_expert * capacity
    hidden = w_out.shape[2]
    expert = lax.axis_index("expert")

    both = lambda *stages: [(s, s) for s in stages]
    core, across = ("expert", 1), ("expert", 2)
    along = both(*[("expert", 1 << k) for k in range(2, n_expert.bit_length() - 1)][::-1])
    sides = [("tensor", 1 << k) for k in range(n_tensor.bit_length() - 1)]
    one, two = sides + [across], [across] + sides
    crossed = list(zip(one, two))
    turned = list(zip(two, one))
    last = both(core)
    late = along + crossed + last
    early = turned + along + last
    mid = along[:1] + turned + along[1:] + last
    orders = dict(p=late, d=early, q=late, r=mid, s=late)
    unit = width // 10
    sizes = dict(p=6 * unit, d=4 * unit, q=10 * unit)
    starts = dict(p=0, d=6 * unit, q=0)
    spans = dict(r=(0, 5 * unit), s=(5 * unit, 10 * unit))
    base = orders["p"]

    scaled = (
        (
            quant_tokens.astype(jnp.float32).reshape(tok_dev, blocks, width // blocks)
            * token_scales[:, :, None]
        )
        .reshape(tok_dev, width)
        .astype(jnp.bfloat16)
    )
    routes = jnp.concatenate([expert_ids.astype(jnp.bfloat16), gate_weights], axis=1)
    routes = jnp.pad(routes, ((0, 0), (0, LANES - 2 * top)))

    rows = {}
    for name in "pdq":
        lo, hi = starts[name], starts[name] + sizes[name]
        part = scaled[:, lo:hi] if name in "pd" else grad_out[:, lo:hi]
        rows[name] = jnp.concatenate([part, routes], axis=1) if name == "d" else part

    tips = {}

    def step(name, *others):
        level = (rows[name].shape[0] // tok_dev).bit_length() - 1
        sent = after(rows[name], *others) if others else rows[name]
        got = swap(sent, orders[name][level])
        tips[name] = sent
        rows[name] = jnp.concatenate([sent, got], axis=0) if level < 3 else (sent, got)
        return got

    def finish(name, *others):
        low, high = rows[name]
        far_low = swap(after(low, *others[:-1]) if others[:-1] else low, last[0])
        far_high = swap(after(high, *others[-1:]) if others else high, last[0])
        rows[name] = (low, high, far_low, far_high)
        return far_high

    def make_routes():
        routes_all = jnp.concatenate([block[:, sizes["d"] :] for block in rows["d"]], axis=0)
        routes_all = jnp.dot(
            order_matrix(orders["d"], base, tok_dev),
            routes_all,
            preferred_element_type=jnp.float32,
        )
        lane = lax.broadcasted_iota(jnp.int32, routes_all.shape, 1)
        named = (routes_all == expert.astype(jnp.float32)) & (lane < top)
        chosen = jnp.any(named, axis=1, keepdims=True)
        gate_lanes = jnp.pad(routes_all[:, top:], ((0, 0), (0, top)))
        token_gate = jnp.sum(jnp.where(named, gate_lanes, 0.0), axis=1, keepdims=True)
        earlier = lax.broadcasted_iota(jnp.int32, (tokens, tokens), 0)
        later = lax.broadcasted_iota(jnp.int32, (tokens, tokens), 1)
        far = 2 * tokens
        ranking = jnp.where(earlier == later, -far, (earlier < later).astype(jnp.int32))
        ranking = ranking.astype(jnp.bfloat16)
        member = chosen.astype(jnp.bfloat16)
        rank = far + lax.dot_general(member, ranking, FIRST, preferred_element_type=jnp.float32)
        slot = lax.broadcasted_iota(jnp.int32, (slots, tokens), 0).astype(jnp.float32)
        placing = (slot == rank).astype(jnp.bfloat16)
        slot_gates = jnp.dot(
            placing, token_gate.astype(jnp.bfloat16), preferred_element_type=jnp.float32
        )
        placings = {}
        for name in orders:
            if orders[name] == base:
                placings[name] = placing
                continue
            moved = order_matrix(orders[name], base, tok_dev)
            placings[name] = jnp.dot(
                placing, moved, preferred_element_type=jnp.float32
            ).astype(jnp.bfloat16)
        return named, slot_gates, placings

    picked = dict(x=(), g=())

    def pick_step(name, *others):
        kind = "x" if name in "pd" else "g"
        place = after(placings[name], *others) if others else placings[name]
        picked[kind] = (
            pick(place, rows[name], sizes[name], starts[name], width, picked[kind]),
        )
        return picked[kind][0]

    def cut(name, *others):
        lo, hi = spans[name]
        return lax.optimization_barrier(after(w_in, *others)[lo:hi, 0])

    halves = {}
    p0 = step("p")
    q0 = step("q", tips["p"])
    d0 = step("d", tips["q"])
    p1 = step("p")
    d1 = step("d", p0)
    d2 = step("d")
    q1 = step("q", p1)
    p2 = step("p")
    halves["r"] = cut("r", tips["p"], tips["q"])
    p3 = step("p", halves["r"])
    d3 = step("d", p2)
    q2 = step("q", d2)
    halves["s"] = cut("s", tips["q"], tips["d"])
    finish("p", halves["s"])
    q3 = step("q", d3, halves["s"])
    finish("d")
    named, slot_gates, placings = make_routes()
    pick_step("p", tips["q"])
    inputs = pick_step("d", tips["q"])
    projected = 0.0
    for name in "rs":
        lo, hi = spans[name]
        projected += jnp.einsum(
            "rd,djh->rjh", inputs[:, lo:hi], halves[name], preferred_element_type=jnp.float32
        )
    gate_pre, up_value = projected[:, 0], projected[:, 1]
    finish("q", tips["q"], projected)
    cotangent = pick_step("q")
    back = jnp.dot(cotangent, w_out[:, 0], preferred_element_type=jnp.float32)

    sigmoid_gate = jax.nn.sigmoid(gate_pre)
    activated = gate_pre * sigmoid_gate
    hidden_value = activated * up_value
    gate_piece = jnp.sum(hidden_value * back, axis=1, keepdims=True).astype(jnp.bfloat16)
    grad_hidden = slot_gates * back
    gate_grad = (
        grad_hidden * up_value * sigmoid_gate * (1.0 + gate_pre * (1.0 - sigmoid_gate))
    ).astype(jnp.bfloat16)
    up_grad = (grad_hidden * activated).astype(jnp.bfloat16)
    scaled_hidden = (slot_gates * hidden_value).astype(jnp.bfloat16)

    grads = ()
    sums = {}

    def grad_step(low, high, *others):
        nonlocal grads
        left = after(gate_grad, *others) if others else gate_grad
        grads = weight_grads(
            inputs, cotangent, left, up_grad, scaled_hidden, low, high - low, grads
        )
        return grads[1]

    grad_both = jnp.stack([gate_grad, up_grad], axis=1)

    def piece_step(name, *others):
        lo, hi = spans[name]
        place = placings[name]
        left = after(grad_both, *others) if others else grad_both
        part = jnp.einsum(
            "rjh,djh->rd", left, halves[name], preferred_element_type=jnp.float32
        ).astype(jnp.bfloat16)
        put = lambda rows, kind: lax.dot_general(
            rows, part, FIRST, preferred_element_type=jnp.float32
        ).astype(kind)
        keep, send = put(place[:, :half], jnp.float32), put(place[:, half:], jnp.bfloat16)
        if name == "s":
            token_piece = lax.dot_general(
                place, gate_piece, FIRST, preferred_element_type=jnp.float32
            )
            extra = jnp.where(named, token_piece, 0.0)
            send = jnp.concatenate([send, extra[half:].astype(jnp.bfloat16)], axis=1)
            sums[name] = ([keep, extra[:half]], send)
        else:
            sums[name] = ([keep], send)
        return send

    def sum_step(name, *others):
        keeps, send = sums[name]
        level = (send.shape[0] // tok_dev).bit_length() - 1
        got = swap(send, orders[name][level])
        got = after(got, *others) if others else got
        count = send.shape[0] // 2
        at, new, out = 0, [], []
        for keep in keeps:
            total = keep + got[:, at : at + keep.shape[1]].astype(jnp.float32)
            at += keep.shape[1]
            new.append(total[:count] if level else total)
            out.append(total[count:].astype(jnp.bfloat16))
        send = (out[0] if len(out) == 1 else jnp.concatenate(out, axis=1)) if level else got
        sums[name] = (new, send)
        return send

    sr = piece_step("r")
    ss = piece_step("s", sr)
    r3 = sum_step("r")
    s3 = sum_step("s")
    g1 = grad_step(0, 7 * unit, s3)
    s2 = sum_step("s", g1)
    r2 = sum_step("r")
    g2 = grad_step(7 * unit, 9 * unit, r2)
    s1 = sum_step("s")
    r1 = sum_step("r", g2)
    g3 = grad_step(9 * unit, 10 * unit, r1)
    s0 = sum_step("s")
    r0 = sum_step("r", g3)
    sum_step("s")
    sum_step("r")

    grad_gates = sums["s"][0][1][:, :top]
    grad_tokens = jnp.concatenate([sums[n][0][0].astype(jnp.bfloat16) for n in "rs"], axis=1)
    return (
        grad_tokens,
        grad_gates,
        grads[0].reshape(width, 1, 2, hidden),
        grads[1].reshape(width, 1, hidden),
    )


def body(*arrays):
    quant_tokens, w_in = arrays[0], arrays[5]
    n_expert, n_tensor = lax.axis_size("expert"), lax.axis_size("tensor")
    whole = lax.axis_size("dp") == 1 and w_in.shape[1] == 1
    doubling = n_tensor == 2 and n_expert >= 8 and n_expert & (n_expert - 1) == 0
    few = quant_tokens.shape[0] * n_expert * n_tensor <= 1024
    tiled = quant_tokens.shape[1] % (10 * 512) == 0
    chosen = gathered_body if whole and doubling and few and tiled else routed_body
    return chosen(*arrays)


def solution(mesh):
    in_specs = (
        P(("dp", "expert", "tensor"), None),
        P(("dp", "expert", "tensor"), None),
        P(("dp", "expert", "tensor"), None),
        P(("dp", "expert", "tensor"), None),
        P(("dp", "expert", "tensor"), None),
        P("dp", "expert", None, "tensor"),
        P("dp", "expert", "tensor"),
    )
    out_specs = (
        P(("dp", "expert", "tensor"), None),
        P(("dp", "expert", "tensor"), None),
        P("dp", "expert", None, "tensor"),
        P("dp", "expert", "tensor"),
    )
    return jax.shard_map(body, mesh=mesh, in_specs=in_specs, out_specs=out_specs, check_vma=False)
```
